128 devices in a mesh: blk: 16 (over x_lo, z, core), kv: 8 (over y, x_hi).
Axes of the slice: x: 4 (x_hi: 2, x_lo: 2; x = x_hi * 2 + x_lo), y: 4, z: 4, core: 2. Of those that a mesh axis runs over, the one named last changes fastest.
Arguments:
- hidden: bfloat16 [4096, 2880], P('blk', 'kv'), may hold values from -6 to 6
- gain_attn: float32 [2880], replicated, may hold values from 0.25 to 1.75
- w_q: bfloat16 [2880, 4096], P(None, 'kv'), may hold values from -0.109375 to 0.109375
- w_k: bfloat16 [2880, 512], P(None, 'kv'), may hold values from -0.109375 to 0.109375
- w_v: bfloat16 [2880, 512], P(None, 'kv'), may hold values from -0.109375 to 0.109375
- sinks: float32 [64], P('kv'), may hold values from 3 to 9
- w_o: bfloat16 [4096, 2880], P('kv'), may hold values from -0.75 to 0.75
- gain_moe: float32 [2880], replicated, may hold values from 0.25 to 1.75
- w_router: bfloat16 [2880, 32], replicated, may hold values from -5.1 to 5.1
- w_gate: bfloat16 [32, 2880, 2880], P('blk', None, 'kv'), may hold values from -0.4375 to 0.4375
- w_up: bfloat16 [32, 2880, 2880], P('blk', None, 'kv'), may hold values from -0.4375 to 0.4375
- w_down: bfloat16 [32, 2880, 2880], P('blk', 'kv'), may hold values from -0.013671875 to 0.013671875
- kv_pool: bfloat16 [256, 128, 1024], P('blk', None, 'kv'), may hold values from -160 to 160
- page_table: int32 [16, 16], P('blk'), may hold values from 0 to 255, as said below
- lengths: int32 [16], P('blk'), may hold values from 1 to 2048, as said below
- routes: int32 [4096, 4], P('blk'), may hold values from 0 to 31, all different within a row; in each aligned block of 256 rows (0 to 255, 256 to 511, ...) at most 48 rows name the same one
Outputs:
- mixed: bfloat16 [4096, 2880], P('blk', 'kv')
The draws below stay inside these ranges and needn't reach their ends.
Inputs may be any that keep to these rules, and one draw needn't show every extreme that they name: `page_table`: row r lists distinct pool pages, except that requests with equal r // 4 share their first pages: the same page numbers, all lying within the cached tokens of every request of the group. A page outside such a shared run belongs to one request only. `lengths`: some request has exactly 2048 cached tokens. `routes`: among the rows of one request no expert is named more than 48 times, a bound that some block reaches.
All inputs are finite; a program needn't handle non-finite values.
Results may differ from the reference program's by a relative error of at most 0.015.
The reference program's roundings to bfloat16 on the way count: a program that leaves them out, or rounds other values in their place, can miss the bound.
Values may be sent and summed in bfloat16 or wider, within the bound.
A program may use at most 128 MiB of HBM per device.

```python
import math
import jax
import jax.numpy as jnp
import numpy as np
from jax import lax

D = 2880
QH = 64
KVH = 8
HD = 64
FF = 2880
TOPK = 4
PAGE = 128
GROUP = 4
TOK = 256
MAXP = 16
REQS = 16
TOKENS = 4096
EXPERTS = 32
POOL = 256
CTX = 2048
CAP = 48
N_KV = 8


def paging(key):
    key_len = jax.random.fold_in(key, 101)
    key_top = jax.random.fold_in(key, 102)
    key_share = jax.random.fold_in(key, 103)
    key_perm = jax.random.fold_in(key, 104)
    lengths_all = jax.random.randint(key_len, (REQS,), 1, CTX + 1)
    longest = jax.random.randint(key_top, (), 0, REQS)
    lengths_all = jnp.where(jnp.arange(REQS) == longest, CTX, lengths_all).astype(jnp.int32)
    groups = REQS // GROUP
    fewest = jnp.min(lengths_all.reshape(groups, GROUP), axis=1) // PAGE
    shared = jax.random.randint(key_share, (groups,), 0, fewest + 1)
    ordering = jax.random.permutation(key_perm, POOL).astype(jnp.int32).reshape(REQS, MAXP)
    leader = jnp.arange(REQS) // GROUP * GROUP
    slot_ids = jnp.arange(MAXP)[None, :]
    common = jnp.repeat(shared, GROUP)[:, None]
    table_rows = jnp.where(slot_ids < common, ordering[leader], ordering)
    return (lengths_all, table_rows.astype(jnp.int32))


def draw_lengths(key, part):
    return paging(key)[0]


def draw_page_table(key, part):
    return paging(key)[1]


def draw_kv_pool(key, part):
    base_vals = jnp.clip(jax.random.normal(key, (POOL, PAGE, KVH * 2 * HD), jnp.float32), -4.0, 4.0)
    return base_vals.astype(jnp.bfloat16)


def draw_w_router(key, part):
    base_vals = jnp.clip(jax.random.normal(key, (D, EXPERTS), jnp.float32), -5.0, 5.0) * D ** (-0.5)
    return base_vals.astype(jnp.bfloat16)


def level_of(key, extent, split, smallest, top_value):
    gain, own = 1.0, jax.random.fold_in(key, 6)
    for position, parts in split:
        steps = jnp.exp(jax.random.uniform(jax.random.fold_in(own, position), (parts,), jnp.float32, smallest / len(split), top_value / len(split)))
        gain = gain * jnp.repeat(steps, extent[position] // parts).reshape([-1 if axis == position else 1 for axis in range(len(extent))])
    return gain


def assign_block(stream_key, own, number, rows, count, top, most, lean):
    ranking = jax.random.permutation(stream_key, count)
    crowded, usual = portions_of(count, rows * top, most, lean, True), portions_of(count, rows * top, most, lean, False)
    places = jnp.arange(count)

    def named(sizes, rotation):
        used = int((sizes > 0).sum())
        fixed = max(1, used // 4)
        passed = fixed + (places - fixed + rotation * (used - fixed)) % max(1, count - fixed)
        return jnp.zeros((count,), jnp.int32).at[ranking[jnp.where(places < fixed, places, passed)]].set(jnp.asarray(sizes, jnp.int32))

    sizes = jnp.where(number % 4 == 0, named(crowded, number // 4), named(usual, number - number // 4 - 1))
    mixed = jax.random.permutation(jax.random.fold_in(own, 3), count)
    donor, taker = mixed[0:count // 2 * 2:2], mixed[1:count // 2 * 2:2]
    margin = jnp.minimum(sizes[donor] - 1, most - sizes[taker]) // 2
    margin = jnp.where((donor == ranking[0]) | (taker == ranking[0]) | (sizes[taker] == 0), 0, jnp.maximum(margin, 0))
    passed = jax.random.randint(jax.random.fold_in(own, 4), (count // 2,), 0, 1 << 20) % (margin + 1)
    sizes = sizes.at[donor].add(-passed).at[taker].add(passed)
    labels = jnp.searchsorted(jnp.cumsum(sizes), jnp.arange(rows * top), side="right").astype(jnp.int32)
    listing = labels.reshape(top, rows).T
    listing = listing[jax.random.permutation(jax.random.fold_in(own, 1), rows)]
    rotation = jax.random.randint(jax.random.fold_in(own, 2), (rows, 1), 0, top)
    return jnp.take_along_axis(listing, (jnp.arange(top)[None, :] + rotation) % top, axis=1)


def portions_of(number_of, total, most, skew, full):
    loads = [(1 << 20) // math.isqrt(grade ** skew) + 1 for grade in range(1, number_of + 1)]
    largest = most if full else min(most, max(-(-total // number_of), total * loads[0] // sum(loads)))
    least = 1 if total - largest >= number_of - 1 else 0
    counts, spare = [largest] + [least] * (number_of - 1), total - largest - least * (number_of - 1)
    while spare > 0:
        movable = [i for i in range(1, number_of) if counts[i] < largest] or [i for i in range(1, number_of) if counts[i] < most]
        mass, budget = sum([loads[i] for i in movable]), spare
        for i in movable:
            addition = min(most - counts[i], max(1, budget * loads[i] // mass), spare)
            counts[i] = counts[i] + addition
            spare = spare - addition
    return np.array(counts)


def normal_values(key, extent, scale, limit, pieces=(), held_as=jnp.bfloat16):
    result = jax.random.normal(key, extent, jnp.float32) * scale
    if len(pieces) > 0:
        result = level_of(key, extent, pieces, -0.22, 0.18) * result
    return jnp.clip(result, min=-limit, max=limit).astype(held_as)


def setup_inputs(seed: int = 0) -> dict:
    keys = jax.random.split(jax.random.key(seed), 17)
    hidden = normal_values(keys[0], (TOKENS, D), 1.0, 6.0, ((0, 16), (1, 8)))
    gain_attn = jnp.clip(1.0 + 0.15 * jax.random.normal(keys[1], (D,), jnp.float32), 0.25, 1.75)
    w_q = normal_values(keys[2], (D, QH * HD), D ** -0.5, 0.109375, ((1, 8),))
    w_k = normal_values(keys[3], (D, KVH * HD), D ** -0.5, 0.109375, ((1, 8),))
    w_v = normal_values(keys[4], (D, KVH * HD), D ** -0.5, 0.109375, ((1, 8),))
    sinks = jnp.clip(3.0 + 6.0 * jax.random.uniform(keys[5], (QH,), jnp.float32) ** level_of(keys[5], (QH,), ((0, 8),), -0.2, 0.2), 3.0, 9.0)
    w_o = normal_values(keys[6], (QH * HD, D), (QH * HD // 64) ** -0.5, 0.75, ((0, 8),))
    gain_moe = jnp.clip(1.0 + 0.15 * jax.random.normal(keys[7], (D,), jnp.float32), 0.25, 1.75)
    w_router = draw_w_router(jax.random.fold_in(keys[16], 71), 0)
    w_gate = normal_values(keys[9], (EXPERTS, D, FF), (D // 16) ** -0.5, 0.4375, ((0, 16), (2, 8)))
    w_up = normal_values(keys[10], (EXPERTS, D, FF), (D // 16) ** -0.5, 0.4375, ((0, 16), (2, 8)))
    w_down = normal_values(keys[11], (EXPERTS, FF, D), (FF * 64) ** -0.5, 0.013671875, ((0, 16), (1, 8)))
    kv_pool = draw_kv_pool(jax.random.fold_in(keys[16], 71), 0)
    page_table = draw_page_table(jax.random.fold_in(keys[16], 71), 0)
    lengths = draw_lengths(jax.random.fold_in(keys[16], 71), 0)
    routes_keys = jax.random.split(jax.random.fold_in(keys[15], 1), TOKENS // TOK)
    routes_turns = jax.random.permutation(jax.random.fold_in(keys[15], 3), TOKENS // TOK)
    routes = jax.vmap(lambda own, number: assign_block(jax.random.fold_in(keys[15], 2), own, number, TOK, EXPERTS, TOPK, CAP, 2))(routes_keys, routes_turns).reshape((TOKENS, TOPK))
    return dict(hidden=hidden, gain_attn=gain_attn, w_q=w_q, w_k=w_k, w_v=w_v, sinks=sinks, w_o=w_o, gain_moe=gain_moe, w_router=w_router, w_gate=w_gate, w_up=w_up, w_down=w_down, kv_pool=kv_pool, page_table=page_table, lengths=lengths, routes=routes)


epsilon = 1e-05
rope_base = 150000.0
clamp_limit = 7.0
glu_alpha = 1.702

def rms_scale(values, gain_vec):
    mean_sq = lax.optimization_barrier(jnp.mean(values * values, axis=-1, keepdims=True))
    return values * lax.rsqrt(mean_sq + epsilon) * gain_vec

def rotate(vectors, positions):
    half_dim = vectors.shape[-1] // 2
    inv_freq = rope_base ** (-jnp.arange(half_dim, dtype=jnp.float32) / half_dim)
    angles = positions.astype(jnp.float32)[:, None] * inv_freq[None, :]
    cosines = jnp.cos(angles)[:, None, :]
    sines = jnp.sin(angles)[:, None, :]
    front_half = vectors[..., :half_dim]
    back_half = vectors[..., half_dim:]
    return jnp.concatenate([front_half * cosines - back_half * sines, back_half * cosines + front_half * sines], axis=-1)

def swiglu(gate_in, up_in):
    gate_in = jnp.minimum(gate_in, clamp_limit)
    up_in = jnp.clip(up_in, -clamp_limit, clamp_limit)
    return (up_in + 1.0) * gate_in * jax.nn.sigmoid(glu_alpha * gate_in)

def attend(normed, length, page_rows, w_q, w_k, w_v, sinks):
    tok_rows = normed.shape[0]
    kv_heads = w_k.shape[1] // HD
    per_group = w_q.shape[1] // w_k.shape[1]
    positions = length + jnp.arange(tok_rows, dtype=jnp.int32)
    queries = jnp.dot(normed, w_q, preferred_element_type=jnp.float32).reshape(tok_rows, kv_heads * per_group, HD)
    queries = rotate(queries, positions).astype(jnp.bfloat16).reshape(tok_rows, kv_heads, per_group, HD)
    key_new = jnp.dot(normed, w_k, preferred_element_type=jnp.float32).reshape(tok_rows, kv_heads, HD)
    key_new = rotate(key_new, positions).astype(jnp.bfloat16)
    value_new = jnp.dot(normed, w_v, preferred_element_type=jnp.float32).astype(jnp.bfloat16).reshape(tok_rows, kv_heads, HD)
    cached = page_rows.reshape(-1, kv_heads, 2, HD)
    ctx_len = cached.shape[0]
    key_all = jnp.concatenate([cached[:, :, 0], key_new], axis=0)
    value_all = jnp.concatenate([cached[:, :, 1], value_new], axis=0)
    row_ids = jnp.arange(tok_rows, dtype=jnp.int32)[:, None]
    col_ids = jnp.arange(ctx_len + tok_rows, dtype=jnp.int32)[None, :]
    visible = jnp.where(col_ids < ctx_len, col_ids < length, col_ids - ctx_len <= row_ids)
    scores = jnp.einsum('tgjd,kgd->gjtk', queries.astype(jnp.float32), key_all.astype(jnp.float32)) * HD ** (-0.5)
    scores = jnp.where(visible[None, None], scores, -jnp.inf)
    sink_term = sinks.reshape(kv_heads, per_group)[:, :, None, None]
    row_top = jnp.maximum(lax.optimization_barrier(jnp.max(scores, axis=-1, keepdims=True)), sink_term)
    exp_terms = jnp.exp(scores - row_top)
    denom_sum = lax.optimization_barrier(jnp.sum(exp_terms, axis=-1, keepdims=True)) + jnp.exp(sink_term - row_top)
    weights_attn = (exp_terms / denom_sum).astype(jnp.bfloat16)
    attended = jnp.einsum('gjtk,kgd->tgjd', weights_attn.astype(jnp.float32), value_all.astype(jnp.float32))
    return attended.astype(jnp.bfloat16).reshape(tok_rows, -1)

def expert_slots(route_rows, expert_count):
    expert_ids = route_rows.reshape(-1)
    one_hot = (expert_ids[:, None] == jnp.arange(expert_count, dtype=jnp.int32)[None, :]).astype(jnp.int32)
    earlier = jnp.cumsum(one_hot, axis=0) - one_hot
    return (expert_ids, lax.optimization_barrier(jnp.sum(earlier * one_hot, axis=1)).astype(jnp.int32))

def reference(hidden, gain_attn, w_q, w_k, w_v, sinks, w_o, gain_moe, w_router, w_gate, w_up, w_down, kv_pool, page_table, lengths, routes):
    states = hidden.astype(jnp.float32)
    normed = rms_scale(states, gain_attn).astype(jnp.bfloat16)

    def one_request(packed):
        block_rows, block_len, block_table = packed
        page_rows = kv_pool[block_table].reshape(MAXP * PAGE, -1)
        return attend(block_rows, block_len, page_rows, w_q, w_k, w_v, sinks)
    attended = lax.map(one_request, (normed.reshape(REQS, TOK, D), lengths, page_table)).reshape(TOKENS, QH * HD)
    residual = states + jnp.dot(attended, w_o, preferred_element_type=jnp.float32)
    moe_in = rms_scale(residual, gain_moe).astype(jnp.bfloat16)
    logits = jnp.dot(moe_in, w_router, preferred_element_type=jnp.float32)
    chosen = jnp.take_along_axis(logits, routes, axis=1)
    weights = jax.nn.softmax(chosen, axis=1)
    expert_ids, slot_ids = jax.vmap(lambda route_rows: expert_slots(route_rows, EXPERTS))(routes.reshape(REQS, TOK, TOPK))
    sources = jnp.arange(REQS, dtype=jnp.int32)[:, None]
    places = ((expert_ids * REQS + sources) * CAP + slot_ids).reshape(-1)
    buffer = jnp.zeros((EXPERTS * REQS * CAP, D), jnp.bfloat16).at[places].set(jnp.repeat(moe_in, TOPK, axis=0))
    buffer = buffer.reshape(EXPERTS, REQS * CAP, D)

    def one_expert(packed):
        slot_rows, gate_w, up_w, down_w = packed
        gate_val = jnp.dot(slot_rows, gate_w, preferred_element_type=jnp.float32)
        up_val = jnp.dot(slot_rows, up_w, preferred_element_type=jnp.float32)
        act = swiglu(gate_val, up_val).astype(jnp.bfloat16)
        blocks = act.reshape(-1, N_KV, FF // N_KV).astype(jnp.float32)
        down_blocks = down_w.reshape(N_KV, FF // N_KV, D).astype(jnp.float32)
        partial_value = jnp.einsum('rsf,sfd->srd', blocks, down_blocks).astype(jnp.bfloat16)
        partial_value = lax.optimization_barrier(partial_value)
        return lax.optimization_barrier(jnp.sum(partial_value.astype(jnp.float32), axis=0))
    outputs = lax.map(one_expert, (buffer, w_gate, w_up, w_down)).reshape(-1, D)
    picked = outputs[places].reshape(TOKENS, TOPK, D)
    mixture = jnp.einsum('tk,tkd->td', weights, picked)
    return (residual + mixture).astype(jnp.bfloat16)
```

```python
import jax
import jax.numpy as jnp
from jax import lax
from jax.sharding import PartitionSpec as P

HD = 64
EXP_DEV = 2


epsilon = 1e-05
rope_base = 150000.0
clamp_limit = 7.0
glu_alpha = 1.702


def rms_scale(values, gain_vec):
    mean_sq = jnp.mean(values * values, axis=-1, keepdims=True)
    return values * lax.rsqrt(mean_sq + epsilon) * gain_vec


def rotate(vectors, positions):
    half_dim = vectors.shape[-1] // 2
    inv_freq = rope_base ** (-jnp.arange(half_dim, dtype=jnp.float32) / half_dim)
    angles = positions.astype(jnp.float32)[:, None] * inv_freq[None, :]
    cosines = jnp.cos(angles)[:, None, :]
    sines = jnp.sin(angles)[:, None, :]
    front_half = vectors[..., :half_dim]
    back_half = vectors[..., half_dim:]
    return jnp.concatenate(
        [front_half * cosines - back_half * sines, back_half * cosines + front_half * sines],
        axis=-1,
    )


def swiglu(gate_in, up_in):
    gate_in = jnp.minimum(gate_in, clamp_limit)
    up_in = jnp.clip(up_in, -clamp_limit, clamp_limit)
    return (up_in + 1.0) * gate_in * jax.nn.sigmoid(glu_alpha * gate_in)


def attend(normed, length, page_rows, w_q, w_k, w_v, sinks):
    tok_rows = normed.shape[0]
    kv_heads = w_k.shape[1] // HD
    per_group = w_q.shape[1] // w_k.shape[1]
    positions = length + jnp.arange(tok_rows, dtype=jnp.int32)
    queries = jnp.dot(normed, w_q, preferred_element_type=jnp.float32).reshape(
        tok_rows, kv_heads * per_group, HD
    )
    queries = (
        rotate(queries, positions).astype(jnp.bfloat16).reshape(tok_rows, kv_heads, per_group, HD)
    )
    key_new = jnp.dot(normed, w_k, preferred_element_type=jnp.float32).reshape(
        tok_rows, kv_heads, HD
    )
    key_new = rotate(key_new, positions).astype(jnp.bfloat16)
    value_new = (
        jnp.dot(normed, w_v, preferred_element_type=jnp.float32)
        .astype(jnp.bfloat16)
        .reshape(tok_rows, kv_heads, HD)
    )
    cached = page_rows.reshape(-1, kv_heads, 2, HD)
    ctx_len = cached.shape[0]
    key_all = jnp.concatenate([cached[:, :, 0], key_new], axis=0)
    value_all = jnp.concatenate([cached[:, :, 1], value_new], axis=0)
    row_ids = jnp.arange(tok_rows, dtype=jnp.int32)[:, None]
    col_ids = jnp.arange(ctx_len + tok_rows, dtype=jnp.int32)[None, :]
    visible = jnp.where(col_ids < ctx_len, col_ids < length, col_ids - ctx_len <= row_ids)
    scores = jnp.einsum(
        "tgjd,kgd->gjtk", queries, key_all, preferred_element_type=jnp.float32
    ) * HD ** (-0.5)
    scores = jnp.where(visible[None, None], scores, -jnp.inf)
    sink_term = sinks.reshape(kv_heads, per_group)[:, :, None, None]
    row_top = jnp.maximum(jnp.max(scores, axis=-1, keepdims=True), sink_term)
    exp_terms = jnp.exp(scores - row_top)
    denom_sum = jnp.sum(exp_terms, axis=-1, keepdims=True) + jnp.exp(sink_term - row_top)
    weights_attn = (exp_terms / denom_sum).astype(jnp.bfloat16)
    attended = jnp.einsum(
        "gjtk,kgd->tgjd", weights_attn, value_all, preferred_element_type=jnp.float32
    )
    return attended.astype(jnp.bfloat16).reshape(tok_rows, -1)


def expert_slots(route_rows, expert_count):
    expert_ids = route_rows.reshape(-1)
    one_hot = (expert_ids[:, None] == jnp.arange(expert_count, dtype=jnp.int32)[None, :]).astype(
        jnp.int32
    )
    earlier = jnp.cumsum(one_hot, axis=0) - one_hot
    return (expert_ids, jnp.sum(earlier * one_hot, axis=1))


def gather_kv(block):
    count = lax.axis_size("kv")
    rows, width = block.shape
    spread = jnp.broadcast_to(block[:, None, :], (rows, count, width))
    return lax.all_to_all(spread, "kv", 1, 1, tiled=True).reshape(rows, count * width)


def reduce_kv(block):
    count = lax.axis_size("kv")
    rows, width = block.shape
    parts = lax.all_to_all(block.reshape(rows, count, width // count), "kv", 1, 1, tiled=True)
    return jnp.sum(parts.astype(jnp.float32), axis=1)


def local(
    hidden,
    gain_attn,
    w_q,
    w_k,
    w_v,
    sinks,
    w_o,
    gain_moe,
    w_router,
    w_gate,
    w_up,
    w_down,
    kv_pool,
    page_table,
    lengths,
    routes,
):
    tok_rows = hidden.shape[0]
    slice_width = hidden.shape[1]
    kv_rank = lax.axis_index("kv")
    full_rows = gather_kv(hidden)
    states = full_rows.astype(jnp.float32)
    normed = rms_scale(states, gain_attn).astype(jnp.bfloat16)
    pool_all = lax.all_gather(kv_pool, "blk", axis=0, tiled=True)
    page_rows = jnp.take(pool_all, page_table[0], axis=0)
    page_rows = page_rows.reshape(page_rows.shape[0] * page_rows.shape[1], -1)
    attended = attend(normed, lengths[0], page_rows, w_q, w_k, w_v, sinks)
    partial_value = jnp.dot(attended, w_o, preferred_element_type=jnp.float32)
    shared = reduce_kv(partial_value.astype(jnp.bfloat16))
    residual_slice = hidden.astype(jnp.float32) + shared
    total_sq = lax.psum(jnp.sum(residual_slice * residual_slice, axis=1), "kv")
    gain_slice = lax.dynamic_slice_in_dim(gain_moe, kv_rank * slice_width, slice_width, 0)
    moe_slice_in = (
        residual_slice
        * lax.rsqrt(total_sq[:, None] / (slice_width * lax.axis_size("kv")) + epsilon)
        * gain_slice
    ).astype(jnp.bfloat16)
    router_rows = lax.dynamic_slice_in_dim(w_router, kv_rank * slice_width, slice_width, 0)
    logits = lax.psum(
        jnp.dot(moe_slice_in, router_rows, preferred_element_type=jnp.float32), "kv"
    )
    weights = jax.nn.softmax(jnp.take_along_axis(logits, routes, axis=1), axis=1)
    top_count = routes.shape[1]
    blk_count = lax.axis_size("blk")
    experts = EXP_DEV * blk_count
    capacity = max(2, 3 * tok_rows * top_count // (2 * experts))
    expert_ids, slot_ids = expert_slots(routes, experts)
    places = (expert_ids * capacity + slot_ids).reshape(tok_rows, top_count)
    slot_index = jnp.arange(experts * capacity, dtype=jnp.int32)
    picks = places[:, :, None] == slot_index[None, None, :]
    dispatch = jnp.any(picks, axis=1).astype(jnp.bfloat16)
    outgoing = jnp.dot(dispatch.T, moe_slice_in, preferred_element_type=jnp.float32).astype(
        jnp.bfloat16
    )
    outgoing = outgoing.reshape(blk_count, EXP_DEV * capacity, slice_width)
    items = lax.all_to_all(outgoing, "blk", 0, 0, tiled=True)
    items = gather_kv(items.reshape(blk_count * EXP_DEV * capacity, slice_width))
    items = items.reshape(blk_count, EXP_DEV, capacity, -1)
    gate_val = jnp.einsum("becd,edf->becf", items, w_gate, preferred_element_type=jnp.float32)
    up_val = jnp.einsum("becd,edf->becf", items, w_up, preferred_element_type=jnp.float32)
    act = swiglu(gate_val, up_val).astype(jnp.bfloat16)
    expert_part = jnp.einsum(
        "becf,efd->becd", act, w_down, preferred_element_type=jnp.float32
    ).astype(jnp.bfloat16)
    expert_out = reduce_kv(expert_part.reshape(blk_count * EXP_DEV * capacity, -1))
    expert_out = expert_out.astype(jnp.bfloat16).reshape(blk_count, EXP_DEV * capacity, slice_width)
    arrived = lax.all_to_all(expert_out, "blk", 0, 0, tiled=True)
    arrived = arrived.reshape(experts * capacity, slice_width)
    picked = jnp.einsum(
        "tkp,pd->tkd", picks.astype(jnp.bfloat16), arrived, preferred_element_type=jnp.float32
    )
    moe_slice = jnp.einsum("tk,tkd->td", weights, picked)
    return (residual_slice + moe_slice).astype(jnp.bfloat16)


def solution(mesh):
    in_specs = (
        P("blk", "kv"),
        P(),
        P(None, "kv"),
        P(None, "kv"),
        P(None, "kv"),
        P("kv"),
        P("kv", None),
        P(),
        P(),
        P("blk", None, "kv"),
        P("blk", None, "kv"),
        P("blk", "kv", None),
        P("blk", None, "kv"),
        P("blk", None),
        P("blk"),
        P("blk", None),
    )
    out_specs = P("blk", "kv")
    return jax.shard_map(local, mesh=mesh, in_specs=in_specs, out_specs=out_specs, check_vma=False)
```

```python
import jax
import jax.numpy as jnp
from jax import lax
from jax.sharding import PartitionSpec as P

HD = 64
EXP_DEV = 2


epsilon = 1e-05
rope_base = 150000.0
clamp_limit = 7.0
glu_alpha = 1.702


def rms_scale(values, gain_vec):
    mean_sq = jnp.mean(values * values, axis=-1, keepdims=True)
    return values * lax.rsqrt(mean_sq + epsilon) * gain_vec


def rotate(vectors, positions):
    half_dim = vectors.shape[-1] // 2
    inv_freq = rope_base ** (-jnp.arange(half_dim, dtype=jnp.float32) / half_dim)
    angles = positions.astype(jnp.float32)[:, None] * inv_freq[None, :]
    cosines = jnp.cos(angles)[:, None, :]
    sines = jnp.sin(angles)[:, None, :]
    front_half = vectors[..., :half_dim]
    back_half = vectors[..., half_dim:]
    return jnp.concatenate(
        [front_half * cosines - back_half * sines, back_half * cosines + front_half * sines],
        axis=-1,
    )


def swiglu(gate_in, up_in):
    gate_in = jnp.minimum(gate_in, clamp_limit)
    up_in = jnp.clip(up_in, -clamp_limit, clamp_limit)
    return (up_in + 1.0) * gate_in * jax.nn.sigmoid(glu_alpha * gate_in)


def attend(normed, length, page_rows, w_q, w_k, w_v, sinks):
    tok_rows = normed.shape[0]
    kv_heads = w_k.shape[1] // HD
    per_group = w_q.shape[1] // w_k.shape[1]
    positions = length + jnp.arange(tok_rows, dtype=jnp.int32)
    queries = jnp.dot(normed, w_q, preferred_element_type=jnp.float32).reshape(
        tok_rows, kv_heads * per_group, HD
    )
    queries = (
        rotate(queries, positions).astype(jnp.bfloat16).reshape(tok_rows, kv_heads, per_group, HD)
    )
    key_new = jnp.dot(normed, w_k, preferred_element_type=jnp.float32).reshape(
        tok_rows, kv_heads, HD
    )
    key_new = rotate(key_new, positions).astype(jnp.bfloat16)
    value_new = (
        jnp.dot(normed, w_v, preferred_element_type=jnp.float32)
        .astype(jnp.bfloat16)
        .reshape(tok_rows, kv_heads, HD)
    )
    cached = page_rows.reshape(-1, kv_heads, 2, HD)
    ctx_len = cached.shape[0]
    key_all = jnp.concatenate([cached[:, :, 0], key_new], axis=0)
    value_all = jnp.concatenate([cached[:, :, 1], value_new], axis=0)
    row_ids = jnp.arange(tok_rows, dtype=jnp.int32)[:, None]
    col_ids = jnp.arange(ctx_len + tok_rows, dtype=jnp.int32)[None, :]
    visible = jnp.where(col_ids < ctx_len, col_ids < length, col_ids - ctx_len <= row_ids)
    scores = jnp.einsum(
        "tgjd,kgd->gjtk", queries, key_all, preferred_element_type=jnp.float32
    ) * HD ** (-0.5)
    scores = jnp.where(visible[None, None], scores, -jnp.inf)
    sink_term = sinks.reshape(kv_heads, per_group)[:, :, None, None]
    row_top = jnp.maximum(jnp.max(scores, axis=-1, keepdims=True), sink_term)
    exp_terms = jnp.exp(scores - row_top)
    denom_sum = jnp.sum(exp_terms, axis=-1, keepdims=True) + jnp.exp(sink_term - row_top)
    weights_attn = (exp_terms / denom_sum).astype(jnp.bfloat16)
    attended = jnp.einsum(
        "gjtk,kgd->tgjd", weights_attn, value_all, preferred_element_type=jnp.float32
    )
    return attended.astype(jnp.bfloat16).reshape(tok_rows, -1)


def expert_slots(route_rows, expert_count):
    expert_ids = route_rows.reshape(-1)
    one_hot = (expert_ids[:, None] == jnp.arange(expert_count, dtype=jnp.int32)[None, :]).astype(
        jnp.int32
    )
    earlier = jnp.cumsum(one_hot, axis=0) - one_hot
    return (expert_ids, jnp.sum(earlier * one_hot, axis=1))


def gather_kv(block):
    count = lax.axis_size("kv")
    spread = jnp.broadcast_to(block[None], (count,) + block.shape)
    return lax.all_to_all(spread, "kv", 0, 0, tiled=True)


def reduce_kv(stacked):
    parts = lax.all_to_all(stacked, "kv", 0, 0, tiled=True)
    return jnp.sum(parts.astype(jnp.float32), axis=0)


def split_columns(block, count):
    rows, width = block.shape
    return block.reshape(rows, count, width // count).transpose(1, 0, 2)


def join_columns(stacked):
    count, rows, width = stacked.shape
    return stacked.transpose(1, 0, 2).reshape(rows, count * width)


def local(
    hidden,
    gain_attn,
    w_q,
    w_k,
    w_v,
    sinks,
    w_o,
    gain_moe,
    w_router,
    w_gate,
    w_up,
    w_down,
    kv_pool,
    page_table,
    lengths,
    routes,
):
    tok_rows = hidden.shape[0]
    slice_width = hidden.shape[1]
    kv_rank = lax.axis_index("kv")
    kv_count = lax.axis_size("kv")
    full_rows = join_columns(gather_kv(hidden))
    states = full_rows.astype(jnp.float32)
    normed = rms_scale(states, gain_attn).astype(jnp.bfloat16)
    pool_all = lax.all_gather(kv_pool, "blk", axis=0, tiled=True)
    page_rows = jnp.take(pool_all, page_table[0], axis=0)
    page_rows = page_rows.reshape(page_rows.shape[0] * page_rows.shape[1], -1)
    attended = attend(normed, lengths[0], page_rows, w_q, w_k, w_v, sinks)
    partial_value = jnp.dot(attended, w_o, preferred_element_type=jnp.float32)
    shared = reduce_kv(split_columns(partial_value.astype(jnp.bfloat16), kv_count))
    residual_slice = hidden.astype(jnp.float32) + shared
    total_sq = lax.psum(jnp.sum(residual_slice * residual_slice, axis=1), "kv")
    gain_slice = lax.dynamic_slice_in_dim(gain_moe, kv_rank * slice_width, slice_width, 0)
    moe_slice_in = (
        residual_slice
        * lax.rsqrt(total_sq[:, None] / (slice_width * lax.axis_size("kv")) + epsilon)
        * gain_slice
    ).astype(jnp.bfloat16)
    router_rows = lax.dynamic_slice_in_dim(w_router, kv_rank * slice_width, slice_width, 0)
    logits = lax.psum(
        jnp.dot(moe_slice_in, router_rows, preferred_element_type=jnp.float32), "kv"
    )
    weights = jax.nn.softmax(jnp.take_along_axis(logits, routes, axis=1), axis=1)
    top_count = routes.shape[1]
    blk_count = lax.axis_size("blk")
    experts = EXP_DEV * blk_count
    capacity = max(2, 3 * tok_rows * top_count // (2 * experts))
    expert_ids, slot_ids = expert_slots(routes, experts)
    places = (expert_ids * capacity + slot_ids).reshape(tok_rows, top_count)
    slot_index = jnp.arange(experts * capacity, dtype=jnp.int32)
    picks = places[:, :, None] == slot_index[None, None, :]
    dispatch = jnp.any(picks, axis=1).astype(jnp.bfloat16)
    outgoing = jnp.dot(dispatch.T, moe_slice_in, preferred_element_type=jnp.float32).astype(
        jnp.bfloat16
    )
    outgoing = outgoing.reshape(blk_count, EXP_DEV * capacity, slice_width)
    weights, outgoing = lax.optimization_barrier((weights, outgoing))
    items = lax.all_to_all(outgoing, "blk", 0, 0, tiled=True)
    items = items.reshape(blk_count, EXP_DEV, capacity, slice_width).transpose(1, 0, 2, 3)
    items = items.reshape(EXP_DEV * blk_count * capacity, slice_width)
    items = join_columns(gather_kv(items)).reshape(EXP_DEV, blk_count * capacity, -1)
    gate_val = jnp.einsum("erd,edf->erf", items, w_gate, preferred_element_type=jnp.float32)
    up_val = jnp.einsum("erd,edf->erf", items, w_up, preferred_element_type=jnp.float32)
    act = swiglu(gate_val, up_val).astype(jnp.bfloat16)
    expert_part = jnp.einsum(
        "erf,efd->erd", act, w_down, preferred_element_type=jnp.float32
    ).astype(jnp.bfloat16)
    expert_part = expert_part.reshape(EXP_DEV * blk_count * capacity, -1)
    expert_out = reduce_kv(split_columns(expert_part, kv_count)).astype(jnp.bfloat16)
    expert_out = expert_out.reshape(EXP_DEV, blk_count, capacity, slice_width).transpose(1, 0, 2, 3)
    expert_out = expert_out.reshape(blk_count, EXP_DEV * capacity, slice_width)
    arrived = lax.all_to_all(expert_out, "blk", 0, 0, tiled=True)
    arrived = arrived.reshape(experts * capacity, slice_width)
    picked = jnp.einsum(
        "tkp,pd->tkd", picks.astype(jnp.bfloat16), arrived, preferred_element_type=jnp.float32
    )
    moe_slice = jnp.einsum("tk,tkd->td", weights, picked)
    return (residual_slice + moe_slice).astype(jnp.bfloat16)


def solution(mesh):
    in_specs = (
        P("blk", "kv"),
        P(),
        P(None, "kv"),
        P(None, "kv"),
        P(None, "kv"),
        P("kv"),
        P("kv", None),
        P(),
        P(),
        P("blk", None, "kv"),
        P("blk", None, "kv"),
        P("blk", "kv", None),
        P("blk", None, "kv"),
        P("blk", None),
        P("blk"),
        P("blk", None),
    )
    out_specs = P("blk", "kv")
    return jax.shard_map(local, mesh=mesh, in_specs=in_specs, out_specs=out_specs, check_vma=False)
```

```python
import jax
import jax.numpy as jnp
from jax import lax
from jax.sharding import PartitionSpec as P

HD = 64
EXP_DEV = 2


epsilon = 1e-05
rope_base = 150000.0
clamp_limit = 7.0
glu_alpha = 1.702


def rms_scale(values, gain_vec):
    mean_sq = jnp.mean(values * values, axis=-1, keepdims=True)
    return values * lax.rsqrt(mean_sq + epsilon) * gain_vec


def rotate(vectors, positions):
    half_dim = vectors.shape[-1] // 2
    inv_freq = rope_base ** (-jnp.arange(half_dim, dtype=jnp.float32) / half_dim)
    angles = positions.astype(jnp.float32)[:, None] * inv_freq[None, :]
    cosines = jnp.cos(angles)[:, None, :]
    sines = jnp.sin(angles)[:, None, :]
    front_half = vectors[..., :half_dim]
    back_half = vectors[..., half_dim:]
    return jnp.concatenate(
        [front_half * cosines - back_half * sines, back_half * cosines + front_half * sines],
        axis=-1,
    )


def swiglu(gate_in, up_in):
    gate_in = jnp.minimum(gate_in, clamp_limit)
    up_in = jnp.clip(up_in, -clamp_limit, clamp_limit)
    return (up_in + 1.0) * gate_in * jax.nn.sigmoid(glu_alpha * gate_in)


def attend(normed, length, page_rows, w_q, w_k, w_v, sinks):
    tok_rows = normed.shape[0]
    kv_heads = w_k.shape[1] // HD
    per_group = w_q.shape[1] // w_k.shape[1]
    positions = length + jnp.arange(tok_rows, dtype=jnp.int32)
    queries = jnp.dot(normed, w_q, preferred_element_type=jnp.float32).reshape(
        tok_rows, kv_heads * per_group, HD
    )
    queries = (
        rotate(queries, positions).astype(jnp.bfloat16).reshape(tok_rows, kv_heads, per_group, HD)
    )
    key_new = jnp.dot(normed, w_k, preferred_element_type=jnp.float32).reshape(
        tok_rows, kv_heads, HD
    )
    key_new = rotate(key_new, positions).astype(jnp.bfloat16)
    value_new = (
        jnp.dot(normed, w_v, preferred_element_type=jnp.float32)
        .astype(jnp.bfloat16)
        .reshape(tok_rows, kv_heads, HD)
    )
    cached = page_rows.reshape(-1, kv_heads, 2, HD)
    ctx_len = cached.shape[0]
    key_all = jnp.concatenate([cached[:, :, 0], key_new], axis=0)
    value_all = jnp.concatenate([cached[:, :, 1], value_new], axis=0)
    row_ids = jnp.arange(tok_rows, dtype=jnp.int32)[:, None]
    col_ids = jnp.arange(ctx_len + tok_rows, dtype=jnp.int32)[None, :]
    visible = jnp.where(col_ids < ctx_len, col_ids < length, col_ids - ctx_len <= row_ids)
    scores = jnp.einsum(
        "tgjd,kgd->gjtk", queries, key_all, preferred_element_type=jnp.float32
    ) * HD ** (-0.5)
    scores = jnp.where(visible[None, None], scores, -jnp.inf)
    sink_term = sinks.reshape(kv_heads, per_group)[:, :, None, None]
    row_top = jnp.maximum(jnp.max(scores, axis=-1, keepdims=True), sink_term)
    exp_terms = jnp.exp(scores - row_top)
    denom_sum = jnp.sum(exp_terms, axis=-1, keepdims=True) + jnp.exp(sink_term - row_top)
    weights_attn = (exp_terms / denom_sum).astype(jnp.bfloat16)
    attended = jnp.einsum(
        "gjtk,kgd->tgjd", weights_attn, value_all, preferred_element_type=jnp.float32
    )
    return attended.astype(jnp.bfloat16).reshape(tok_rows, -1)


def expert_slots(route_rows, expert_count):
    expert_ids = route_rows.reshape(-1)
    one_hot = (expert_ids[:, None] == jnp.arange(expert_count, dtype=jnp.int32)[None, :]).astype(
        jnp.int32
    )
    earlier = jnp.cumsum(one_hot, axis=0) - one_hot
    return (expert_ids, jnp.sum(earlier * one_hot, axis=1))


def gather_kv(block):
    count = lax.axis_size("kv")
    spread = jnp.broadcast_to(block[None], (count,) + block.shape)
    return lax.all_to_all(spread, "kv", 0, 0, tiled=True)


def reduce_kv(stacked):
    parts = lax.all_to_all(stacked, "kv", 0, 0, tiled=True)
    return jnp.sum(parts.astype(jnp.float32), axis=0)


def split_columns(block, count):
    rows, width = block.shape
    return block.reshape(rows, count, width // count).transpose(1, 0, 2)


def join_columns(stacked):
    count, rows, width = stacked.shape
    return stacked.transpose(1, 0, 2).reshape(rows, count * width)


def widen_rows(weight, count, pad):
    lead, depth, width = weight.shape
    weight = weight.reshape(lead, count, depth // count, width)
    weight = jnp.pad(weight, ((0, 0), (0, 0), (0, pad), (0, 0)))
    return weight.reshape(lead, count * (depth // count + pad), width)


def widen_cols(weight, count, pad):
    lead, depth, width = weight.shape
    weight = weight.reshape(lead, depth, count, width // count)
    weight = jnp.pad(weight, ((0, 0), (0, 0), (0, 0), (0, pad)))
    return weight.reshape(lead, depth, count * (width // count + pad))


def local(
    hidden,
    gain_attn,
    w_q,
    w_k,
    w_v,
    sinks,
    w_o,
    gain_moe,
    w_router,
    w_gate,
    w_up,
    w_down,
    kv_pool,
    page_table,
    lengths,
    routes,
):
    tok_rows = hidden.shape[0]
    slice_width = hidden.shape[1]
    kv_rank = lax.axis_index("kv")
    kv_count = lax.axis_size("kv")
    full_rows = join_columns(gather_kv(hidden))
    states = full_rows.astype(jnp.float32)
    normed = rms_scale(states, gain_attn).astype(jnp.bfloat16)
    pool_all = lax.all_gather(kv_pool, "blk", axis=0, tiled=True)
    page_rows = jnp.take(pool_all, page_table[0], axis=0)
    page_rows = page_rows.reshape(page_rows.shape[0] * page_rows.shape[1], -1)
    attended = attend(normed, lengths[0], page_rows, w_q, w_k, w_v, sinks)
    partial_value = jnp.dot(attended, w_o, preferred_element_type=jnp.float32)
    shared = reduce_kv(split_columns(partial_value.astype(jnp.bfloat16), kv_count))
    residual_slice = hidden.astype(jnp.float32) + shared
    total_sq = lax.psum(jnp.sum(residual_slice * residual_slice, axis=1), "kv")
    gain_slice = lax.dynamic_slice_in_dim(gain_moe, kv_rank * slice_width, slice_width, 0)
    moe_slice_in = (
        residual_slice
        * lax.rsqrt(total_sq[:, None] / (slice_width * lax.axis_size("kv")) + epsilon)
        * gain_slice
    ).astype(jnp.bfloat16)
    top_count = routes.shape[1]
    blk_count = lax.axis_size("blk")
    blk_rank = lax.axis_index("blk")
    experts = EXP_DEV * blk_count
    capacity = max(2, 3 * tok_rows * top_count // (2 * experts))
    slots = experts * capacity
    pad = (-slice_width) % 128
    wide = slice_width + pad
    expert_ids, slot_ids = expert_slots(routes, experts)
    places = (expert_ids * capacity + slot_ids).reshape(tok_rows, top_count)
    slot_index = jnp.arange(slots, dtype=jnp.int32)
    picks = places[:, :, None] == slot_index[None, None, :]
    dispatch = jnp.any(picks, axis=1).astype(jnp.bfloat16)
    moe_wide = jnp.pad(moe_slice_in, ((0, 0), (0, pad)))
    outgoing = jnp.dot(dispatch.T, moe_wide, preferred_element_type=jnp.float32).astype(
        jnp.bfloat16
    )
    outgoing = outgoing.reshape(blk_count, EXP_DEV * capacity, wide)
    items = lax.all_to_all(outgoing, "blk", 0, 0, tiled=True)
    items = items.reshape(blk_count, EXP_DEV, capacity, wide).transpose(1, 0, 2, 3)
    items = gather_kv(items.reshape(slots, wide))
    items = items.transpose(1, 0, 2).reshape(EXP_DEV, blk_count * capacity, kv_count * wide)
    gate_val = jnp.einsum(
        "erk,ekf->erf", items, widen_rows(w_gate, kv_count, pad), preferred_element_type=jnp.float32
    )
    up_val = jnp.einsum(
        "erk,ekf->erf", items, widen_rows(w_up, kv_count, pad), preferred_element_type=jnp.float32
    )
    act = swiglu(gate_val, up_val).astype(jnp.bfloat16)
    expert_part = jnp.einsum(
        "erf,efk->erk", act, widen_cols(w_down, kv_count, pad), preferred_element_type=jnp.float32
    ).astype(jnp.bfloat16)
    expert_part = expert_part.reshape(slots, kv_count, wide).transpose(1, 0, 2)
    expert_out = reduce_kv(expert_part)[:, :slice_width].astype(jnp.bfloat16)
    router_cols = lax.dynamic_slice_in_dim(w_router, blk_rank * EXP_DEV, EXP_DEV, 1)
    router_cols = widen_rows(router_cols.T[:, :, None], kv_count, pad)[:, :, 0]
    chosen = jnp.einsum("erk,ek->er", items, router_cols, preferred_element_type=jnp.float32)
    chosen = chosen.reshape(slots, 1)
    high = chosen.astype(jnp.bfloat16)
    rest = chosen - high.astype(jnp.float32)
    middle = rest.astype(jnp.bfloat16)
    low = (rest - middle.astype(jnp.float32)).astype(jnp.bfloat16)
    filler = jnp.zeros((slots, pad - 3), jnp.bfloat16)
    expert_out = jnp.concatenate([expert_out, high, middle, low, filler], axis=1)
    expert_out = expert_out.reshape(EXP_DEV, blk_count, capacity, wide).transpose(1, 0, 2, 3)
    expert_out = expert_out.reshape(blk_count, EXP_DEV * capacity, wide)
    arrived = lax.all_to_all(expert_out, "blk", 0, 0, tiled=True)
    arrived = arrived.reshape(slots, wide)
    picked = jnp.einsum(
        "tkp,pd->tkd", picks.astype(jnp.bfloat16), arrived, preferred_element_type=jnp.float32
    )
    logits = (
        picked[:, :, slice_width] + picked[:, :, slice_width + 1]
    ) + picked[:, :, slice_width + 2]
    weights = jax.nn.softmax(logits, axis=1)
    moe_slice = jnp.einsum("tk,tkd->td", weights, picked[:, :, :slice_width])
    return (residual_slice + moe_slice).astype(jnp.bfloat16)


def solution(mesh):
    in_specs = (
        P("blk", "kv"),
        P(),
        P(None, "kv"),
        P(None, "kv"),
        P(None, "kv"),
        P("kv"),
        P("kv", None),
        P(),
        P(),
        P("blk", None, "kv"),
        P("blk", None, "kv"),
        P("blk", "kv", None),
        P("blk", None, "kv"),
        P("blk", None),
        P("blk"),
        P("blk", None),
    )
    out_specs = P("blk", "kv")
    return jax.shard_map(local, mesh=mesh, in_specs=in_specs, out_specs=out_specs, check_vma=False)
```

```python
import jax
import jax.numpy as jnp
from jax import lax
from jax.sharding import PartitionSpec as P

HD = 64
EXP_DEV = 2


epsilon = 1e-05
rope_base = 150000.0
clamp_limit = 7.0
glu_alpha = 1.702


def rms_scale(values, gain_vec):
    mean_sq = jnp.mean(values * values, axis=-1, keepdims=True)
    return values * lax.rsqrt(mean_sq + epsilon) * gain_vec


def rotate(vectors, positions):
    half_dim = vectors.shape[-1] // 2
    inv_freq = rope_base ** (-jnp.arange(half_dim, dtype=jnp.float32) / half_dim)
    angles = positions.astype(jnp.float32)[:, None] * inv_freq[None, :]
    cosines = jnp.cos(angles)[:, None, :]
    sines = jnp.sin(angles)[:, None, :]
    front_half = vectors[..., :half_dim]
    back_half = vectors[..., half_dim:]
    return jnp.concatenate(
        [front_half * cosines - back_half * sines, back_half * cosines + front_half * sines],
        axis=-1,
    )


def swiglu(gate_in, up_in):
    gate_in = jnp.minimum(gate_in, clamp_limit)
    up_in = jnp.clip(up_in, -clamp_limit, clamp_limit)
    return (up_in + 1.0) * gate_in * jax.nn.sigmoid(glu_alpha * gate_in)


def attend(normed, length, page_rows, w_q, w_k, w_v, sinks):
    tok_rows = normed.shape[0]
    kv_heads = w_k.shape[1] // HD
    per_group = w_q.shape[1] // w_k.shape[1]
    positions = length + jnp.arange(tok_rows, dtype=jnp.int32)
    queries = jnp.dot(normed, w_q, preferred_element_type=jnp.float32).reshape(
        tok_rows, kv_heads * per_group, HD
    )
    queries = (
        rotate(queries, positions).astype(jnp.bfloat16).reshape(tok_rows, kv_heads, per_group, HD)
    )
    key_new = jnp.dot(normed, w_k, preferred_element_type=jnp.float32).reshape(
        tok_rows, kv_heads, HD
    )
    key_new = rotate(key_new, positions).astype(jnp.bfloat16)
    value_new = (
        jnp.dot(normed, w_v, preferred_element_type=jnp.float32)
        .astype(jnp.bfloat16)
        .reshape(tok_rows, kv_heads, HD)
    )
    cached = page_rows.reshape(-1, kv_heads, 2, HD)
    ctx_len = cached.shape[0]
    key_all = jnp.concatenate([cached[:, :, 0], key_new], axis=0)
    value_all = jnp.concatenate([cached[:, :, 1], value_new], axis=0)
    row_ids = jnp.arange(tok_rows, dtype=jnp.int32)[:, None]
    col_ids = jnp.arange(ctx_len + tok_rows, dtype=jnp.int32)[None, :]
    visible = jnp.where(col_ids < ctx_len, col_ids < length, col_ids - ctx_len <= row_ids)
    scores = jnp.einsum(
        "tgjd,kgd->gjtk", queries, key_all, preferred_element_type=jnp.float32
    ) * HD ** (-0.5)
    scores = jnp.where(visible[None, None], scores, -jnp.inf)
    sink_term = sinks.reshape(kv_heads, per_group)[:, :, None, None]
    row_top = jnp.maximum(jnp.max(scores, axis=-1, keepdims=True), sink_term)
    exp_terms = jnp.exp(scores - row_top)
    denom_sum = jnp.sum(exp_terms, axis=-1, keepdims=True) + jnp.exp(sink_term - row_top)
    weights_attn = (exp_terms / denom_sum).astype(jnp.bfloat16)
    attended = jnp.einsum(
        "gjtk,kgd->tgjd", weights_attn, value_all, preferred_element_type=jnp.float32
    )
    return attended.astype(jnp.bfloat16).reshape(tok_rows, -1)


def expert_slots(route_rows, expert_count):
    expert_ids = route_rows.reshape(-1)
    one_hot = (expert_ids[:, None] == jnp.arange(expert_count, dtype=jnp.int32)[None, :]).astype(
        jnp.int32
    )
    earlier = jnp.cumsum(one_hot, axis=0) - one_hot
    return (expert_ids, jnp.sum(earlier * one_hot, axis=1))


def gather_kv(block):
    count = lax.axis_size("kv")
    spread = jnp.broadcast_to(block[None], (count,) + block.shape)
    return lax.all_to_all(spread, "kv", 0, 0, tiled=True)


def reduce_kv(stacked):
    parts = lax.all_to_all(stacked, "kv", 0, 0, tiled=True)
    return jnp.sum(parts.astype(jnp.float32), axis=0)


def split_columns(block, count):
    rows, width = block.shape
    return block.reshape(rows, count, width // count).transpose(1, 0, 2)


def join_columns(stacked):
    count, rows, width = stacked.shape
    return stacked.transpose(1, 0, 2).reshape(rows, count * width)


def widen_rows(weight, count, pad):
    lead, depth, width = weight.shape
    weight = weight.reshape(lead, count, depth // count, width)
    weight = jnp.pad(weight, ((0, 0), (0, 0), (0, pad), (0, 0)))
    return weight.reshape(lead, count * (depth // count + pad), width)


def widen_cols(weight, count, pad):
    lead, depth, width = weight.shape
    weight = weight.reshape(lead, depth, count, width // count)
    weight = jnp.pad(weight, ((0, 0), (0, 0), (0, 0), (0, pad)))
    return weight.reshape(lead, depth, count * (width // count + pad))


def local(
    hidden,
    gain_attn,
    w_q,
    w_k,
    w_v,
    sinks,
    w_o,
    gain_moe,
    w_router,
    w_gate,
    w_up,
    w_down,
    kv_pool,
    page_table,
    lengths,
    routes,
):
    tok_rows = hidden.shape[0]
    slice_width = hidden.shape[1]
    kv_rank = lax.axis_index("kv")
    kv_count = lax.axis_size("kv")
    full_rows = join_columns(gather_kv(hidden))
    states = full_rows.astype(jnp.float32)
    normed = rms_scale(states, gain_attn).astype(jnp.bfloat16)
    pool_all = lax.all_gather(kv_pool, "blk", axis=0, tiled=True)
    page_rows = jnp.take(pool_all, page_table[0], axis=0)
    page_rows = page_rows.reshape(page_rows.shape[0] * page_rows.shape[1], -1)
    attended = attend(normed, lengths[0], page_rows, w_q, w_k, w_v, sinks)
    partial_value = jnp.dot(attended, w_o, preferred_element_type=jnp.float32)
    shared = reduce_kv(split_columns(partial_value.astype(jnp.bfloat16), kv_count))
    residual_slice = hidden.astype(jnp.float32) + shared
    total_sq = lax.psum(jnp.sum(residual_slice * residual_slice, axis=1), "kv")
    gain_slice = lax.dynamic_slice_in_dim(gain_moe, kv_rank * slice_width, slice_width, 0)
    moe_slice_in = (
        residual_slice
        * lax.rsqrt(total_sq[:, None] / (slice_width * lax.axis_size("kv")) + epsilon)
        * gain_slice
    ).astype(jnp.bfloat16)
    top_count = routes.shape[1]
    blk_count = lax.axis_size("blk")
    blk_rank = lax.axis_index("blk")
    experts = EXP_DEV * blk_count
    capacity = max(2, 3 * tok_rows * top_count // (2 * experts))
    slots = experts * capacity
    pad = (-slice_width) % 128
    wide = slice_width + pad
    expert_ids, slot_ids = expert_slots(routes, experts)
    places = (expert_ids * capacity + slot_ids).reshape(tok_rows, top_count)
    slot_index = jnp.arange(slots, dtype=jnp.int32)
    picks = places[:, :, None] == slot_index[None, None, :]
    dispatch = jnp.any(picks, axis=1).astype(jnp.bfloat16)
    moe_wide = jnp.pad(moe_slice_in, ((0, 0), (0, pad)))
    outgoing = jnp.dot(dispatch.T, moe_wide, preferred_element_type=jnp.float32).astype(
        jnp.bfloat16
    )
    outgoing = outgoing.reshape(blk_count, EXP_DEV * capacity, wide)
    items = lax.all_to_all(outgoing, "blk", 0, 0, tiled=True)
    items = items.reshape(blk_count, EXP_DEV, capacity, wide).transpose(1, 0, 2, 3)
    items = gather_kv(items.reshape(slots, wide))
    items = items.reshape(kv_count, EXP_DEV, blk_count * capacity, wide)
    gate_w = widen_rows(w_gate, kv_count, pad).reshape(EXP_DEV, kv_count, wide, -1)
    up_w = widen_rows(w_up, kv_count, pad).reshape(EXP_DEV, kv_count, wide, -1)
    gate_val = jnp.einsum("ierd,eidf->erf", items, gate_w, preferred_element_type=jnp.float32)
    up_val = jnp.einsum("ierd,eidf->erf", items, up_w, preferred_element_type=jnp.float32)
    act = swiglu(gate_val, up_val).astype(jnp.bfloat16)
    down_w = widen_cols(w_down, kv_count, pad).reshape(EXP_DEV, -1, kv_count, wide)
    expert_part = jnp.einsum(
        "erf,efid->ierd", act, down_w, preferred_element_type=jnp.float32
    ).astype(jnp.bfloat16)
    expert_part = expert_part.reshape(kv_count, slots, wide)
    expert_out = reduce_kv(expert_part)[:, :slice_width].astype(jnp.bfloat16)
    router_cols = lax.dynamic_slice_in_dim(w_router, blk_rank * EXP_DEV, EXP_DEV, 1)
    router_cols = widen_rows(router_cols.T[:, :, None], kv_count, pad)[:, :, 0]
    router_cols = router_cols.reshape(EXP_DEV, kv_count, wide)
    chosen = jnp.einsum("ierd,eid->er", items, router_cols, preferred_element_type=jnp.float32)
    chosen = chosen.reshape(slots, 1)
    high = chosen.astype(jnp.bfloat16)
    rest = chosen - high.astype(jnp.float32)
    middle = rest.astype(jnp.bfloat16)
    low = (rest - middle.astype(jnp.float32)).astype(jnp.bfloat16)
    filler = jnp.zeros((slots, pad - 3), jnp.bfloat16)
    expert_out = jnp.concatenate([expert_out, high, middle, low, filler], axis=1)
    expert_out = expert_out.reshape(EXP_DEV, blk_count, capacity, wide).transpose(1, 0, 2, 3)
    expert_out = expert_out.reshape(blk_count, EXP_DEV * capacity, wide)
    arrived = lax.all_to_all(expert_out, "blk", 0, 0, tiled=True)
    arrived = arrived.reshape(slots, wide)
    picked = jnp.einsum(
        "tkp,pd->tkd", picks.astype(jnp.bfloat16), arrived, preferred_element_type=jnp.float32
    )
    logits = (
        picked[:, :, slice_width] + picked[:, :, slice_width + 1]
    ) + picked[:, :, slice_width + 2]
    weights = jax.nn.softmax(logits, axis=1)
    moe_slice = jnp.einsum("tk,tkd->td", weights, picked[:, :, :slice_width])
    return (residual_slice + moe_slice).astype(jnp.bfloat16)


def solution(mesh):
    in_specs = (
        P("blk", "kv"),
        P(),
        P(None, "kv"),
        P(None, "kv"),
        P(None, "kv"),
        P("kv"),
        P("kv", None),
        P(),
        P(),
        P("blk", None, "kv"),
        P("blk", None, "kv"),
        P("blk", "kv", None),
        P("blk", None, "kv"),
        P("blk", None),
        P("blk"),
        P("blk", None),
    )
    out_specs = P("blk", "kv")
    return jax.shard_map(local, mesh=mesh, in_specs=in_specs, out_specs=out_specs, check_vma=False)
```

```python
import jax
import jax.numpy as jnp
from jax import lax
from jax.sharding import PartitionSpec as P

HD = 64
EXP_DEV = 2


epsilon = 1e-05
rope_base = 150000.0
clamp_limit = 7.0
glu_alpha = 1.702


def rms_scale(values, gain_vec):
    mean_sq = jnp.mean(values * values, axis=-1, keepdims=True)
    return values * lax.rsqrt(mean_sq + epsilon) * gain_vec


def rotate(vectors, positions):
    half_dim = vectors.shape[-1] // 2
    inv_freq = rope_base ** (-jnp.arange(half_dim, dtype=jnp.float32) / half_dim)
    angles = positions.astype(jnp.float32)[:, None] * inv_freq[None, :]
    cosines = jnp.cos(angles)[:, None, :]
    sines = jnp.sin(angles)[:, None, :]
    front_half = vectors[..., :half_dim]
    back_half = vectors[..., half_dim:]
    return jnp.concatenate(
        [front_half * cosines - back_half * sines, back_half * cosines + front_half * sines],
        axis=-1,
    )


def swiglu(gate_in, up_in):
    gate_in = jnp.minimum(gate_in, clamp_limit)
    up_in = jnp.clip(up_in, -clamp_limit, clamp_limit)
    return (up_in + 1.0) * gate_in * jax.nn.sigmoid(glu_alpha * gate_in)


def attend(normed, length, page_rows, w_q, w_k, w_v, sinks):
    tok_rows = normed.shape[0]
    kv_heads = w_k.shape[1] // HD
    per_group = w_q.shape[1] // w_k.shape[1]
    positions = length + jnp.arange(tok_rows, dtype=jnp.int32)
    queries = jnp.dot(normed, w_q, preferred_element_type=jnp.float32).reshape(
        tok_rows, kv_heads * per_group, HD
    )
    queries = (
        rotate(queries, positions).astype(jnp.bfloat16).reshape(tok_rows, kv_heads, per_group, HD)
    )
    key_new = jnp.dot(normed, w_k, preferred_element_type=jnp.float32).reshape(
        tok_rows, kv_heads, HD
    )
    key_new = rotate(key_new, positions).astype(jnp.bfloat16)
    value_new = (
        jnp.dot(normed, w_v, preferred_element_type=jnp.float32)
        .astype(jnp.bfloat16)
        .reshape(tok_rows, kv_heads, HD)
    )
    cached = page_rows.reshape(-1, kv_heads, 2, HD)
    ctx_len = cached.shape[0]
    key_all = jnp.concatenate([cached[:, :, 0], key_new], axis=0)
    value_all = jnp.concatenate([cached[:, :, 1], value_new], axis=0)
    row_ids = jnp.arange(tok_rows, dtype=jnp.int32)[:, None]
    col_ids = jnp.arange(ctx_len + tok_rows, dtype=jnp.int32)[None, :]
    visible = jnp.where(col_ids < ctx_len, col_ids < length, col_ids - ctx_len <= row_ids)
    scores = jnp.einsum(
        "tgjd,kgd->gjtk", queries, key_all, preferred_element_type=jnp.float32
    ) * HD ** (-0.5)
    scores = jnp.where(visible[None, None], scores, -jnp.inf)
    sink_term = sinks.reshape(kv_heads, per_group)[:, :, None, None]
    row_top = jnp.maximum(jnp.max(scores, axis=-1, keepdims=True), sink_term)
    exp_terms = jnp.exp(scores - row_top)
    denom_sum = jnp.sum(exp_terms, axis=-1, keepdims=True) + jnp.exp(sink_term - row_top)
    weights_attn = (exp_terms / denom_sum).astype(jnp.bfloat16)
    attended = jnp.einsum(
        "gjtk,kgd->tgjd", weights_attn, value_all, preferred_element_type=jnp.float32
    )
    return attended.astype(jnp.bfloat16).reshape(tok_rows, -1)


def expert_slots(route_rows, expert_count):
    expert_ids = route_rows.reshape(-1)
    one_hot = (expert_ids[:, None] == jnp.arange(expert_count, dtype=jnp.int32)[None, :]).astype(
        jnp.int32
    )
    earlier = jnp.cumsum(one_hot, axis=0) - one_hot
    return (expert_ids, jnp.sum(earlier * one_hot, axis=1))


def gather_kv(block):
    count = lax.axis_size("kv")
    spread = jnp.broadcast_to(block[None], (count,) + block.shape)
    return lax.all_to_all(spread, "kv", 0, 0, tiled=True)


def reduce_kv(stacked):
    parts = lax.all_to_all(stacked, "kv", 0, 0, tiled=True)
    return jnp.sum(parts.astype(jnp.float32), axis=0)


def split_columns(block, count):
    rows, width = block.shape
    return block.reshape(rows, count, width // count).transpose(1, 0, 2)


def join_columns(stacked):
    count, rows, width = stacked.shape
    return stacked.transpose(1, 0, 2).reshape(rows, count * width)


def widen_rows(weight, count, pad):
    lead, depth, width = weight.shape
    weight = weight.reshape(lead, count, depth // count, width)
    weight = jnp.pad(weight, ((0, 0), (0, 0), (0, pad), (0, 0)))
    return weight.reshape(lead, count * (depth // count + pad), width)


def widen_cols(weight, count, pad):
    lead, depth, width = weight.shape
    weight = weight.reshape(lead, depth, count, width // count)
    weight = jnp.pad(weight, ((0, 0), (0, 0), (0, 0), (0, pad)))
    return weight.reshape(lead, depth, count * (width // count + pad))


def local(
    hidden,
    gain_attn,
    w_q,
    w_k,
    w_v,
    sinks,
    w_o,
    gain_moe,
    w_router,
    w_gate,
    w_up,
    w_down,
    kv_pool,
    page_table,
    lengths,
    routes,
):
    tok_rows = hidden.shape[0]
    slice_width = hidden.shape[1]
    kv_rank = lax.axis_index("kv")
    kv_count = lax.axis_size("kv")
    full_rows = join_columns(gather_kv(hidden))
    states = full_rows.astype(jnp.float32)
    normed = rms_scale(states, gain_attn).astype(jnp.bfloat16)
    pool_all = lax.all_gather(kv_pool, "blk", axis=0, tiled=True)
    page_rows = jnp.take(pool_all, page_table[0], axis=0)
    page_rows = page_rows.reshape(page_rows.shape[0] * page_rows.shape[1], -1)
    attended = attend(normed, lengths[0], page_rows, w_q, w_k, w_v, sinks)
    partial_value = jnp.dot(attended, w_o, preferred_element_type=jnp.float32)
    shared = reduce_kv(split_columns(partial_value.astype(jnp.bfloat16), kv_count))
    residual_slice = hidden.astype(jnp.float32) + shared
    total_sq = lax.psum(jnp.sum(residual_slice * residual_slice, axis=1), "kv")
    gain_slice = lax.dynamic_slice_in_dim(gain_moe, kv_rank * slice_width, slice_width, 0)
    moe_slice_in = (
        residual_slice
        * lax.rsqrt(total_sq[:, None] / (slice_width * lax.axis_size("kv")) + epsilon)
        * gain_slice
    ).astype(jnp.bfloat16)
    top_count = routes.shape[1]
    blk_count = lax.axis_size("blk")
    blk_rank = lax.axis_index("blk")
    experts = EXP_DEV * blk_count
    capacity = max(2, 3 * tok_rows * top_count // (2 * experts))
    slots = experts * capacity
    pad = (-slice_width) % 128
    wide = slice_width + pad
    expert_ids, slot_ids = expert_slots(routes, experts)
    places = (expert_ids * capacity + slot_ids).reshape(tok_rows, top_count)
    slot_index = jnp.arange(slots, dtype=jnp.int32)
    picks = places[:, :, None] == slot_index[None, None, :]
    dispatch = jnp.any(picks, axis=1).astype(jnp.bfloat16)
    moe_wide = jnp.pad(moe_slice_in, ((0, 0), (0, pad)))
    outgoing = jnp.dot(dispatch.T, moe_wide, preferred_element_type=jnp.float32).astype(
        jnp.bfloat16
    )
    outgoing = outgoing.reshape(blk_count, EXP_DEV * capacity, wide)
    items = lax.all_to_all(outgoing, "blk", 0, 0, tiled=True)
    items = items.reshape(blk_count, EXP_DEV, capacity, wide).transpose(1, 0, 2, 3)
    items = items.reshape(EXP_DEV, blk_count * capacity, wide)
    gate_w = widen_rows(w_gate, kv_count, pad).reshape(EXP_DEV, kv_count, wide, -1)
    up_w = widen_rows(w_up, kv_count, pad).reshape(EXP_DEV, kv_count, wide, -1)
    down_w = widen_cols(w_down, kv_count, pad).reshape(EXP_DEV, -1, kv_count, wide)
    router_cols = lax.dynamic_slice_in_dim(w_router, blk_rank * EXP_DEV, EXP_DEV, 1)
    router_cols = widen_rows(router_cols.T[:, :, None], kv_count, pad)[:, :, 0]
    router_cols = router_cols.reshape(EXP_DEV, kv_count, wide)
    outs, chosen = [], []
    for el in range(EXP_DEV):
        with jax.named_scope(f"expert_{el}"):
            rows = gather_kv(items[el])
            gate_val = jnp.einsum("ird,idf->rf", rows, gate_w[el], preferred_element_type=jnp.float32)
            up_val = jnp.einsum("ird,idf->rf", rows, up_w[el], preferred_element_type=jnp.float32)
            act = swiglu(gate_val, up_val).astype(jnp.bfloat16)
            part = jnp.einsum(
                "rf,fid->ird", act, down_w[el], preferred_element_type=jnp.float32
            ).astype(jnp.bfloat16)
            outs.append(reduce_kv(part)[:, :slice_width].astype(jnp.bfloat16))
            chosen.append(
                jnp.einsum("ird,id->r", rows, router_cols[el], preferred_element_type=jnp.float32)
            )
    expert_out = jnp.concatenate(outs, axis=0)
    chosen = jnp.concatenate(chosen, axis=0).reshape(slots, 1)
    high = chosen.astype(jnp.bfloat16)
    rest = chosen - high.astype(jnp.float32)
    middle = rest.astype(jnp.bfloat16)
    low = (rest - middle.astype(jnp.float32)).astype(jnp.bfloat16)
    filler = jnp.zeros((slots, pad - 3), jnp.bfloat16)
    expert_out = jnp.concatenate([expert_out, high, middle, low, filler], axis=1)
    expert_out = expert_out.reshape(EXP_DEV, blk_count, capacity, wide).transpose(1, 0, 2, 3)
    expert_out = expert_out.reshape(blk_count, EXP_DEV * capacity, wide)
    arrived = lax.all_to_all(expert_out, "blk", 0, 0, tiled=True)
    arrived = arrived.reshape(slots, wide)
    picked = jnp.einsum(
        "tkp,pd->tkd", picks.astype(jnp.bfloat16), arrived, preferred_element_type=jnp.float32
    )
    logits = (
        picked[:, :, slice_width] + picked[:, :, slice_width + 1]
    ) + picked[:, :, slice_width + 2]
    weights = jax.nn.softmax(logits, axis=1)
    moe_slice = jnp.einsum("tk,tkd->td", weights, picked[:, :, :slice_width])
    return (residual_slice + moe_slice).astype(jnp.bfloat16)


def solution(mesh):
    in_specs = (
        P("blk", "kv"),
        P(),
        P(None, "kv"),
        P(None, "kv"),
        P(None, "kv"),
        P("kv"),
        P("kv", None),
        P(),
        P(),
        P("blk", None, "kv"),
        P("blk", None, "kv"),
        P("blk", "kv", None),
        P("blk", None, "kv"),
        P("blk", None),
        P("blk"),
        P("blk", None),
    )
    out_specs = P("blk", "kv")
    return jax.shard_map(local, mesh=mesh, in_specs=in_specs, out_specs=out_specs, check_vma=False)
```

```python
import jax
import jax.numpy as jnp
from jax import lax
from jax.sharding import PartitionSpec as P

HD = 64
EXP_DEV = 2


epsilon = 1e-05
rope_base = 150000.0
clamp_limit = 7.0
glu_alpha = 1.702


def rms_scale(values, gain_vec):
    mean_sq = jnp.mean(values * values, axis=-1, keepdims=True)
    return values * lax.rsqrt(mean_sq + epsilon) * gain_vec


def rotate(vectors, positions):
    half_dim = vectors.shape[-1] // 2
    inv_freq = rope_base ** (-jnp.arange(half_dim, dtype=jnp.float32) / half_dim)
    angles = positions.astype(jnp.float32)[:, None] * inv_freq[None, :]
    cosines = jnp.cos(angles)[:, None, :]
    sines = jnp.sin(angles)[:, None, :]
    front_half = vectors[..., :half_dim]
    back_half = vectors[..., half_dim:]
    return jnp.concatenate(
        [front_half * cosines - back_half * sines, back_half * cosines + front_half * sines],
        axis=-1,
    )


def swiglu(gate_in, up_in):
    gate_in = jnp.minimum(gate_in, clamp_limit)
    up_in = jnp.clip(up_in, -clamp_limit, clamp_limit)
    return (up_in + 1.0) * gate_in * jax.nn.sigmoid(glu_alpha * gate_in)


def attend(normed, length, page_rows, w_q, w_k, w_v, sinks):
    tok_rows = normed.shape[0]
    kv_heads = w_k.shape[1] // HD
    per_group = w_q.shape[1] // w_k.shape[1]
    positions = length + jnp.arange(tok_rows, dtype=jnp.int32)
    queries = jnp.dot(normed, w_q, preferred_element_type=jnp.float32).reshape(
        tok_rows, kv_heads * per_group, HD
    )
    queries = (
        rotate(queries, positions).astype(jnp.bfloat16).reshape(tok_rows, kv_heads, per_group, HD)
    )
    key_new = jnp.dot(normed, w_k, preferred_element_type=jnp.float32).reshape(
        tok_rows, kv_heads, HD
    )
    key_new = rotate(key_new, positions).astype(jnp.bfloat16)
    value_new = (
        jnp.dot(normed, w_v, preferred_element_type=jnp.float32)
        .astype(jnp.bfloat16)
        .reshape(tok_rows, kv_heads, HD)
    )
    cached = page_rows.reshape(-1, kv_heads, 2, HD)
    ctx_len = cached.shape[0]
    key_all = jnp.concatenate([cached[:, :, 0], key_new], axis=0)
    value_all = jnp.concatenate([cached[:, :, 1], value_new], axis=0)
    row_ids = jnp.arange(tok_rows, dtype=jnp.int32)[:, None]
    col_ids = jnp.arange(ctx_len + tok_rows, dtype=jnp.int32)[None, :]
    visible = jnp.where(col_ids < ctx_len, col_ids < length, col_ids - ctx_len <= row_ids)
    scores = jnp.einsum(
        "tgjd,kgd->gjtk", queries, key_all, preferred_element_type=jnp.float32
    ) * HD ** (-0.5)
    scores = jnp.where(visible[None, None], scores, -jnp.inf)
    sink_term = sinks.reshape(kv_heads, per_group)[:, :, None, None]
    row_top = jnp.maximum(jnp.max(scores, axis=-1, keepdims=True), sink_term)
    exp_terms = jnp.exp(scores - row_top)
    denom_sum = jnp.sum(exp_terms, axis=-1, keepdims=True) + jnp.exp(sink_term - row_top)
    weights_attn = (exp_terms / denom_sum).astype(jnp.bfloat16)
    attended = jnp.einsum(
        "gjtk,kgd->tgjd", weights_attn, value_all, preferred_element_type=jnp.float32
    )
    return attended.astype(jnp.bfloat16).reshape(tok_rows, -1)


def expert_slots(route_rows, expert_count):
    expert_ids = route_rows.reshape(-1)
    one_hot = (expert_ids[:, None] == jnp.arange(expert_count, dtype=jnp.int32)[None, :]).astype(
        jnp.int32
    )
    earlier = jnp.cumsum(one_hot, axis=0) - one_hot
    return (expert_ids, jnp.sum(earlier * one_hot, axis=1))


def gather_kv(block):
    count = lax.axis_size("kv")
    spread = jnp.broadcast_to(block[None], (count,) + block.shape)
    return lax.all_to_all(spread, "kv", 0, 0, tiled=True)


def reduce_kv(stacked):
    parts = lax.all_to_all(stacked, "kv", 0, 0, tiled=True)
    return jnp.sum(parts.astype(jnp.float32), axis=0)


def split_columns(block, count):
    rows, width = block.shape
    return block.reshape(rows, count, width // count).transpose(1, 0, 2)


def join_columns(stacked):
    count, rows, width = stacked.shape
    return stacked.transpose(1, 0, 2).reshape(rows, count * width)


def widen_rows(weight, count, pad):
    lead, depth, width = weight.shape
    weight = weight.reshape(lead, count, depth // count, width)
    weight = jnp.pad(weight, ((0, 0), (0, 0), (0, pad), (0, 0)))
    return weight.reshape(lead, count * (depth // count + pad), width)


def widen_cols(weight, count, pad):
    lead, depth, width = weight.shape
    weight = weight.reshape(lead, depth, count, width // count)
    weight = jnp.pad(weight, ((0, 0), (0, 0), (0, 0), (0, pad)))
    return weight.reshape(lead, depth, count * (width // count + pad))


def local(
    hidden,
    gain_attn,
    w_q,
    w_k,
    w_v,
    sinks,
    w_o,
    gain_moe,
    w_router,
    w_gate,
    w_up,
    w_down,
    kv_pool,
    page_table,
    lengths,
    routes,
):
    tok_rows = hidden.shape[0]
    slice_width = hidden.shape[1]
    kv_rank = lax.axis_index("kv")
    kv_count = lax.axis_size("kv")
    full_rows = join_columns(gather_kv(hidden))
    states = full_rows.astype(jnp.float32)
    normed = rms_scale(states, gain_attn).astype(jnp.bfloat16)
    pool_all = lax.all_gather(kv_pool, "blk", axis=0, tiled=True)
    page_rows = jnp.take(pool_all, page_table[0], axis=0)
    page_rows = page_rows.reshape(page_rows.shape[0] * page_rows.shape[1], -1)
    attended = attend(normed, lengths[0], page_rows, w_q, w_k, w_v, sinks)
    partial_value = jnp.dot(attended, w_o, preferred_element_type=jnp.float32)
    shared = reduce_kv(split_columns(partial_value.astype(jnp.bfloat16), kv_count))
    residual_slice = hidden.astype(jnp.float32) + shared
    total_sq = lax.psum(jnp.sum(residual_slice * residual_slice, axis=1), "kv")
    gain_slice = lax.dynamic_slice_in_dim(gain_moe, kv_rank * slice_width, slice_width, 0)
    moe_slice_in = (
        residual_slice
        * lax.rsqrt(total_sq[:, None] / (slice_width * lax.axis_size("kv")) + epsilon)
        * gain_slice
    ).astype(jnp.bfloat16)
    top_count = routes.shape[1]
    blk_count = lax.axis_size("blk")
    blk_rank = lax.axis_index("blk")
    experts = EXP_DEV * blk_count
    capacity = max(2, 3 * tok_rows * top_count // (2 * experts))
    slots = experts * capacity
    pad = (-slice_width) % 128
    wide = slice_width + pad
    expert_ids, slot_ids = expert_slots(routes, experts)
    places = (expert_ids * capacity + slot_ids).reshape(tok_rows, top_count)
    slot_index = jnp.arange(slots, dtype=jnp.int32)
    picks = places[:, :, None] == slot_index[None, None, :]
    dispatch = jnp.any(picks, axis=1).astype(jnp.bfloat16)
    moe_wide = jnp.pad(moe_slice_in, ((0, 0), (0, pad)))
    outgoing = jnp.dot(dispatch.T, moe_wide, preferred_element_type=jnp.float32).astype(
        jnp.bfloat16
    )
    outgoing = outgoing.reshape(blk_count, EXP_DEV, capacity, wide)
    gate_w = widen_rows(w_gate, kv_count, pad).reshape(EXP_DEV, kv_count, wide, -1)
    up_w = widen_rows(w_up, kv_count, pad).reshape(EXP_DEV, kv_count, wide, -1)
    down_w = widen_cols(w_down, kv_count, pad).reshape(EXP_DEV, -1, kv_count, wide)
    router_cols = lax.dynamic_slice_in_dim(w_router, blk_rank * EXP_DEV, EXP_DEV, 1)
    router_cols = widen_rows(router_cols.T[:, :, None], kv_count, pad)[:, :, 0]
    router_cols = router_cols.reshape(EXP_DEV, kv_count, wide)
    outs = []
    for el in range(EXP_DEV):
        with jax.named_scope(f"expert_{el}"):
            items = lax.all_to_all(outgoing[:, el], "blk", 0, 0, tiled=True)
            rows = gather_kv(items.reshape(blk_count * capacity, wide))
            gate_val = jnp.einsum("ird,idf->rf", rows, gate_w[el], preferred_element_type=jnp.float32)
            up_val = jnp.einsum("ird,idf->rf", rows, up_w[el], preferred_element_type=jnp.float32)
            act = swiglu(gate_val, up_val).astype(jnp.bfloat16)
            part = jnp.einsum(
                "rf,fid->ird", act, down_w[el], preferred_element_type=jnp.float32
            ).astype(jnp.bfloat16)
            out_el = reduce_kv(part)[:, :slice_width].astype(jnp.bfloat16)
            chosen_el = jnp.einsum(
                "ird,id->r", rows, router_cols[el], preferred_element_type=jnp.float32
            )
            chosen = chosen_el.reshape(blk_count * capacity, 1)
            high = chosen.astype(jnp.bfloat16)
            rest = chosen - high.astype(jnp.float32)
            middle = rest.astype(jnp.bfloat16)
            low = (rest - middle.astype(jnp.float32)).astype(jnp.bfloat16)
            filler = jnp.zeros((blk_count * capacity, pad - 3), jnp.bfloat16)
            back = jnp.concatenate([out_el, high, middle, low, filler], axis=1)
            back = back.reshape(blk_count, capacity, wide)
            outs.append(lax.all_to_all(back, "blk", 0, 0, tiled=True))
    arrived = jnp.stack(outs, axis=1).reshape(slots, wide)
    picked = jnp.einsum(
        "tkp,pd->tkd", picks.astype(jnp.bfloat16), arrived, preferred_element_type=jnp.float32
    )
    logits = (
        picked[:, :, slice_width] + picked[:, :, slice_width + 1]
    ) + picked[:, :, slice_width + 2]
    weights = jax.nn.softmax(logits, axis=1)
    moe_slice = jnp.einsum("tk,tkd->td", weights, picked[:, :, :slice_width])
    return (residual_slice + moe_slice).astype(jnp.bfloat16)


def solution(mesh):
    in_specs = (
        P("blk", "kv"),
        P(),
        P(None, "kv"),
        P(None, "kv"),
        P(None, "kv"),
        P("kv"),
        P("kv", None),
        P(),
        P(),
        P("blk", None, "kv"),
        P("blk", None, "kv"),
        P("blk", "kv", None),
        P("blk", None, "kv"),
        P("blk", None),
        P("blk"),
        P("blk", None),
    )
    out_specs = P("blk", "kv")
    return jax.shard_map(local, mesh=mesh, in_specs=in_specs, out_specs=out_specs, check_vma=False)
```

```python
import jax
import jax.numpy as jnp
from jax import lax
from jax.sharding import PartitionSpec as P

HD = 64
EXP_DEV = 2


epsilon = 1e-05
rope_base = 150000.0
clamp_limit = 7.0
glu_alpha = 1.702


def rms_scale(values, gain_vec):
    mean_sq = jnp.mean(values * values, axis=-1, keepdims=True)
    return values * lax.rsqrt(mean_sq + epsilon) * gain_vec


def rotate(vectors, positions):
    half_dim = vectors.shape[-1] // 2
    inv_freq = rope_base ** (-jnp.arange(half_dim, dtype=jnp.float32) / half_dim)
    angles = positions.astype(jnp.float32)[:, None] * inv_freq[None, :]
    cosines = jnp.cos(angles)[:, None, :]
    sines = jnp.sin(angles)[:, None, :]
    front_half = vectors[..., :half_dim]
    back_half = vectors[..., half_dim:]
    return jnp.concatenate(
        [front_half * cosines - back_half * sines, back_half * cosines + front_half * sines],
        axis=-1,
    )


def swiglu(gate_in, up_in):
    gate_in = jnp.minimum(gate_in, clamp_limit)
    up_in = jnp.clip(up_in, -clamp_limit, clamp_limit)
    return (up_in + 1.0) * gate_in * jax.nn.sigmoid(glu_alpha * gate_in)


def attend(normed, length, page_rows, w_q, w_k, w_v, sinks):
    tok_rows = normed.shape[0]
    kv_heads = w_k.shape[1] // HD
    per_group = w_q.shape[1] // w_k.shape[1]
    positions = length + jnp.arange(tok_rows, dtype=jnp.int32)
    queries = jnp.dot(normed, w_q, preferred_element_type=jnp.float32).reshape(
        tok_rows, kv_heads * per_group, HD
    )
    queries = (
        rotate(queries, positions).astype(jnp.bfloat16).reshape(tok_rows, kv_heads, per_group, HD)
    )
    key_new = jnp.dot(normed, w_k, preferred_element_type=jnp.float32).reshape(
        tok_rows, kv_heads, HD
    )
    key_new = rotate(key_new, positions).astype(jnp.bfloat16)
    value_new = (
        jnp.dot(normed, w_v, preferred_element_type=jnp.float32)
        .astype(jnp.bfloat16)
        .reshape(tok_rows, kv_heads, HD)
    )
    cached = page_rows.reshape(-1, kv_heads, 2, HD)
    ctx_len = cached.shape[0]
    key_all = jnp.concatenate([cached[:, :, 0], key_new], axis=0)
    value_all = jnp.concatenate([cached[:, :, 1], value_new], axis=0)
    row_ids = jnp.arange(tok_rows, dtype=jnp.int32)[:, None]
    col_ids = jnp.arange(ctx_len + tok_rows, dtype=jnp.int32)[None, :]
    visible = jnp.where(col_ids < ctx_len, col_ids < length, col_ids - ctx_len <= row_ids)
    scores = jnp.einsum(
        "tgjd,kgd->gjtk", queries, key_all, preferred_element_type=jnp.float32
    ) * HD ** (-0.5)
    scores = jnp.where(visible[None, None], scores, -jnp.inf)
    sink_term = sinks.reshape(kv_heads, per_group)[:, :, None, None]
    row_top = jnp.maximum(jnp.max(scores, axis=-1, keepdims=True), sink_term)
    exp_terms = jnp.exp(scores - row_top)
    denom_sum = jnp.sum(exp_terms, axis=-1, keepdims=True) + jnp.exp(sink_term - row_top)
    weights_attn = (exp_terms / denom_sum).astype(jnp.bfloat16)
    attended = jnp.einsum(
        "gjtk,kgd->tgjd", weights_attn, value_all, preferred_element_type=jnp.float32
    )
    return attended.astype(jnp.bfloat16).reshape(tok_rows, -1)


def expert_slots(route_rows, expert_count):
    expert_ids = route_rows.reshape(-1)
    one_hot = (expert_ids[:, None] == jnp.arange(expert_count, dtype=jnp.int32)[None, :]).astype(
        jnp.int32
    )
    earlier = jnp.cumsum(one_hot, axis=0) - one_hot
    return (expert_ids, jnp.sum(earlier * one_hot, axis=1))


def gather_kv(block):
    count = lax.axis_size("kv")
    spread = jnp.broadcast_to(block[None], (count,) + block.shape)
    return lax.all_to_all(spread, "kv", 0, 0, tiled=True)


def reduce_kv(stacked):
    parts = lax.all_to_all(stacked, "kv", 0, 0, tiled=True)
    return jnp.sum(parts.astype(jnp.float32), axis=0)


def split_columns(block, count):
    rows, width = block.shape
    return block.reshape(rows, count, width // count).transpose(1, 0, 2)


def join_columns(stacked):
    count, rows, width = stacked.shape
    return stacked.transpose(1, 0, 2).reshape(rows, count * width)


def widen_rows(weight, count, pad):
    lead, depth, width = weight.shape
    weight = weight.reshape(lead, count, depth // count, width)
    weight = jnp.pad(weight, ((0, 0), (0, 0), (0, pad), (0, 0)))
    return weight.reshape(lead, count * (depth // count + pad), width)


def widen_cols(weight, count, pad):
    lead, depth, width = weight.shape
    weight = weight.reshape(lead, depth, count, width // count)
    weight = jnp.pad(weight, ((0, 0), (0, 0), (0, 0), (0, pad)))
    return weight.reshape(lead, depth, count * (width // count + pad))


def local(
    hidden,
    gain_attn,
    w_q,
    w_k,
    w_v,
    sinks,
    w_o,
    gain_moe,
    w_router,
    w_gate,
    w_up,
    w_down,
    kv_pool,
    page_table,
    lengths,
    routes,
):
    tok_rows = hidden.shape[0]
    slice_width = hidden.shape[1]
    kv_rank = lax.axis_index("kv")
    kv_count = lax.axis_size("kv")
    full_rows = join_columns(gather_kv(hidden))
    states = full_rows.astype(jnp.float32)
    normed = rms_scale(states, gain_attn).astype(jnp.bfloat16)
    pool_all = lax.all_gather(kv_pool, "blk", axis=0, tiled=True)
    page_rows = jnp.take(pool_all, page_table[0], axis=0)
    page_rows = page_rows.reshape(page_rows.shape[0] * page_rows.shape[1], -1)
    attended = attend(normed, lengths[0], page_rows, w_q, w_k, w_v, sinks)
    partial_value = jnp.dot(attended, w_o, preferred_element_type=jnp.float32)
    shared = reduce_kv(split_columns(partial_value.astype(jnp.bfloat16), kv_count))
    residual_slice = hidden.astype(jnp.float32) + shared
    total_sq = jnp.sum(gather_kv(jnp.sum(residual_slice * residual_slice, axis=1)), axis=0)
    gain_slice = lax.dynamic_slice_in_dim(gain_moe, kv_rank * slice_width, slice_width, 0)
    moe_slice_in = (
        residual_slice
        * lax.rsqrt(total_sq[:, None] / (slice_width * lax.axis_size("kv")) + epsilon)
        * gain_slice
    ).astype(jnp.bfloat16)
    top_count = routes.shape[1]
    blk_count = lax.axis_size("blk")
    blk_rank = lax.axis_index("blk")
    experts = EXP_DEV * blk_count
    capacity = max(2, 3 * tok_rows * top_count // (2 * experts))
    slots = experts * capacity
    pad = (-slice_width) % 128
    wide = slice_width + pad
    expert_ids, slot_ids = expert_slots(routes, experts)
    places = (expert_ids * capacity + slot_ids).reshape(tok_rows, top_count)
    slot_index = jnp.arange(slots, dtype=jnp.int32)
    picks = places[:, :, None] == slot_index[None, None, :]
    dispatch = jnp.any(picks, axis=1).astype(jnp.bfloat16)
    moe_wide = jnp.pad(moe_slice_in, ((0, 0), (0, pad)))
    outgoing = jnp.dot(dispatch.T, moe_wide, preferred_element_type=jnp.float32).astype(
        jnp.bfloat16
    )
    outgoing = outgoing.reshape(blk_count, EXP_DEV * capacity, wide)
    items = lax.all_to_all(outgoing, "blk", 0, 0, tiled=True)
    items = items.reshape(blk_count, EXP_DEV, capacity, wide).transpose(1, 0, 2, 3)
    items = items.reshape(EXP_DEV, blk_count * capacity, wide)
    gate_w = widen_rows(w_gate, kv_count, pad).reshape(EXP_DEV, kv_count, wide, -1)
    up_w = widen_rows(w_up, kv_count, pad).reshape(EXP_DEV, kv_count, wide, -1)
    down_w = widen_cols(w_down, kv_count, pad).reshape(EXP_DEV, -1, kv_count, wide)
    router_cols = lax.dynamic_slice_in_dim(w_router, blk_rank * EXP_DEV, EXP_DEV, 1)
    router_cols = widen_rows(router_cols.T[:, :, None], kv_count, pad)[:, :, 0]
    router_cols = router_cols.reshape(EXP_DEV, kv_count, wide)
    outs, chosen = [], []
    for el in range(EXP_DEV):
        with jax.named_scope(f"expert_{el}"):
            rows = gather_kv(items[el])
            gate_val = jnp.einsum("ird,idf->rf", rows, gate_w[el], preferred_element_type=jnp.float32)
            up_val = jnp.einsum("ird,idf->rf", rows, up_w[el], preferred_element_type=jnp.float32)
            act = swiglu(gate_val, up_val).astype(jnp.bfloat16)
            part = jnp.einsum(
                "rf,fid->ird", act, down_w[el], preferred_element_type=jnp.float32
            ).astype(jnp.bfloat16)
            outs.append(reduce_kv(part)[:, :slice_width].astype(jnp.bfloat16))
            chosen.append(
                jnp.einsum("ird,id->r", rows, router_cols[el], preferred_element_type=jnp.float32)
            )
    expert_out = jnp.concatenate(outs, axis=0)
    chosen = jnp.concatenate(chosen, axis=0).reshape(slots, 1)
    high = chosen.astype(jnp.bfloat16)
    rest = chosen - high.astype(jnp.float32)
    middle = rest.astype(jnp.bfloat16)
    low = (rest - middle.astype(jnp.float32)).astype(jnp.bfloat16)
    filler = jnp.zeros((slots, pad - 3), jnp.bfloat16)
    expert_out = jnp.concatenate([expert_out, high, middle, low, filler], axis=1)
    expert_out = expert_out.reshape(EXP_DEV, blk_count, capacity, wide).transpose(1, 0, 2, 3)
    expert_out = expert_out.reshape(blk_count, EXP_DEV * capacity, wide)
    arrived = lax.all_to_all(expert_out, "blk", 0, 0, tiled=True)
    arrived = arrived.reshape(slots, wide)
    picked = jnp.einsum(
        "tkp,pd->tkd", picks.astype(jnp.bfloat16), arrived, preferred_element_type=jnp.float32
    )
    logits = (
        picked[:, :, slice_width] + picked[:, :, slice_width + 1]
    ) + picked[:, :, slice_width + 2]
    weights = jax.nn.softmax(logits, axis=1)
    moe_slice = jnp.einsum("tk,tkd->td", weights, picked[:, :, :slice_width])
    return (residual_slice + moe_slice).astype(jnp.bfloat16)


def solution(mesh):
    in_specs = (
        P("blk", "kv"),
        P(),
        P(None, "kv"),
        P(None, "kv"),
        P(None, "kv"),
        P("kv"),
        P("kv", None),
        P(),
        P(),
        P("blk", None, "kv"),
        P("blk", None, "kv"),
        P("blk", "kv", None),
        P("blk", None, "kv"),
        P("blk", None),
        P("blk"),
        P("blk", None),
    )
    out_specs = P("blk", "kv")
    return jax.shard_map(local, mesh=mesh, in_specs=in_specs, out_specs=out_specs, check_vma=False)
```

```python
import jax
import jax.numpy as jnp
from jax import lax
from jax.sharding import PartitionSpec as P
from jax.experimental import pallas as pl
from jax.experimental.pallas import tpu as pltpu

HD = 64
EXP_DEV = 2


epsilon = 1e-05
rope_base = 150000.0
clamp_limit = 7.0
glu_alpha = 1.702


def rms_scale(values, gain_vec):
    mean_sq = jnp.mean(values * values, axis=-1, keepdims=True)
    return values * lax.rsqrt(mean_sq + epsilon) * gain_vec


def rotate(vectors, positions):
    half_dim = vectors.shape[-1] // 2
    inv_freq = rope_base ** (-jnp.arange(half_dim, dtype=jnp.float32) / half_dim)
    angles = positions.astype(jnp.float32)[:, None] * inv_freq[None, :]
    cosines = jnp.cos(angles)[:, None, :]
    sines = jnp.sin(angles)[:, None, :]
    front_half = vectors[..., :half_dim]
    back_half = vectors[..., half_dim:]
    return jnp.concatenate(
        [front_half * cosines - back_half * sines, back_half * cosines + front_half * sines],
        axis=-1,
    )


def swiglu(gate_in, up_in):
    gate_in = jnp.minimum(gate_in, clamp_limit)
    up_in = jnp.clip(up_in, -clamp_limit, clamp_limit)
    return (up_in + 1.0) * gate_in * jax.nn.sigmoid(glu_alpha * gate_in)


def head_kernel(len_ref, sink_ref, q_ref, k_ref, v_ref, o_ref):
    head = pl.program_id(0)
    length = len_ref[0]
    scores = lax.dot_general(
        q_ref[0], k_ref[...], (((1,), (1,)), ((), ())), preferred_element_type=jnp.float32
    ) * HD ** (-0.5)
    tok_rows, key_count = scores.shape
    ctx_len = key_count - tok_rows
    row_ids = lax.broadcasted_iota(jnp.int32, scores.shape, 0)
    col_ids = lax.broadcasted_iota(jnp.int32, scores.shape, 1)
    cached_seen = (col_ids < ctx_len) & (col_ids < length)
    new_seen = (col_ids >= ctx_len) & (col_ids - ctx_len <= row_ids)
    scores = jnp.where(cached_seen | new_seen, scores, -jnp.inf)
    sink = sink_ref[head]
    row_top = jnp.maximum(jnp.max(scores, axis=1, keepdims=True), sink)
    exp_terms = jnp.exp(scores - row_top)
    denom_sum = jnp.sum(exp_terms, axis=1, keepdims=True) + jnp.exp(sink - row_top)
    weights_attn = (exp_terms / denom_sum).astype(jnp.bfloat16)
    o_ref[0] = jnp.dot(weights_attn, v_ref[...], preferred_element_type=jnp.float32).astype(
        o_ref.dtype
    )


def attend(normed, length, page_rows, w_q, w_k, w_v, sinks):
    tok_rows = normed.shape[0]
    heads = w_q.shape[1] // HD
    positions = length + jnp.arange(tok_rows, dtype=jnp.int32)
    queries = jnp.dot(normed, w_q, preferred_element_type=jnp.float32).reshape(tok_rows, heads, HD)
    queries = rotate(queries, positions).astype(jnp.bfloat16).transpose(1, 0, 2)
    key_new = jnp.dot(normed, w_k, preferred_element_type=jnp.float32).reshape(tok_rows, 1, HD)
    key_new = rotate(key_new, positions).astype(jnp.bfloat16).reshape(tok_rows, HD)
    value_new = jnp.dot(normed, w_v, preferred_element_type=jnp.float32).astype(jnp.bfloat16)
    cached = page_rows.reshape(-1, 2, HD)
    key_all = jnp.concatenate([cached[:, 0], key_new], axis=0)
    value_all = jnp.concatenate([cached[:, 1], value_new], axis=0)
    keys = key_all.shape[0]
    attended = pl.pallas_call(
        head_kernel,
        out_shape=jax.ShapeDtypeStruct((heads, tok_rows, HD), jnp.bfloat16),
        grid_spec=pltpu.PrefetchScalarGridSpec(
            num_scalar_prefetch=2,
            grid=(heads,),
            in_specs=[
                pl.BlockSpec((1, tok_rows, HD), lambda h, n, s: (h, 0, 0)),
                pl.BlockSpec((keys, HD), lambda h, n, s: (0, 0)),
                pl.BlockSpec((keys, HD), lambda h, n, s: (0, 0)),
            ],
            out_specs=pl.BlockSpec((1, tok_rows, HD), lambda h, n, s: (h, 0, 0)),
        ),
        cost_estimate=pl.CostEstimate(
            flops=4 * heads * tok_rows * keys * HD,
            transcendentals=heads * tok_rows * keys,
            bytes_accessed=2 * (2 * heads * tok_rows * HD + 2 * keys * HD),
        ),
    )(length.reshape(1), sinks, queries, key_all, value_all)
    return attended.transpose(1, 0, 2).reshape(tok_rows, heads * HD)


def expert_slots(route_rows, expert_count):
    expert_ids = route_rows.reshape(-1)
    one_hot = (expert_ids[:, None] == jnp.arange(expert_count, dtype=jnp.int32)[None, :]).astype(
        jnp.int32
    )
    earlier = jnp.cumsum(one_hot, axis=0) - one_hot
    return (expert_ids, jnp.sum(earlier * one_hot, axis=1))


def gather_kv(block):
    count = lax.axis_size("kv")
    spread = jnp.broadcast_to(block[None], (count,) + block.shape)
    return lax.all_to_all(spread, "kv", 0, 0, tiled=True)


def reduce_kv(stacked):
    parts = lax.all_to_all(stacked, "kv", 0, 0, tiled=True)
    return jnp.sum(parts.astype(jnp.float32), axis=0)


def split_columns(block, count):
    rows, width = block.shape
    return block.reshape(rows, count, width // count).transpose(1, 0, 2)


def join_columns(stacked):
    count, rows, width = stacked.shape
    return stacked.transpose(1, 0, 2).reshape(rows, count * width)


def widen_rows(weight, count, pad):
    lead, depth, width = weight.shape
    weight = weight.reshape(lead, count, depth // count, width)
    weight = jnp.pad(weight, ((0, 0), (0, 0), (0, pad), (0, 0)))
    return weight.reshape(lead, count * (depth // count + pad), width)


def widen_cols(weight, count, pad):
    lead, depth, width = weight.shape
    weight = weight.reshape(lead, depth, count, width // count)
    weight = jnp.pad(weight, ((0, 0), (0, 0), (0, 0), (0, pad)))
    return weight.reshape(lead, depth, count * (width // count + pad))


def local(
    hidden,
    gain_attn,
    w_q,
    w_k,
    w_v,
    sinks,
    w_o,
    gain_moe,
    w_router,
    w_gate,
    w_up,
    w_down,
    kv_pool,
    page_table,
    lengths,
    routes,
):
    tok_rows = hidden.shape[0]
    slice_width = hidden.shape[1]
    kv_rank = lax.axis_index("kv")
    kv_count = lax.axis_size("kv")
    full_rows = join_columns(gather_kv(hidden))
    states = full_rows.astype(jnp.float32)
    normed = rms_scale(states, gain_attn).astype(jnp.bfloat16)
    pool_all = lax.all_gather(kv_pool, "blk", axis=0, tiled=True)
    page_rows = jnp.take(pool_all, page_table[0], axis=0)
    page_rows = page_rows.reshape(page_rows.shape[0] * page_rows.shape[1], -1)
    attended = attend(normed, lengths[0], page_rows, w_q, w_k, w_v, sinks)
    partial_value = jnp.dot(attended, w_o, preferred_element_type=jnp.float32)
    shared = reduce_kv(split_columns(partial_value.astype(jnp.bfloat16), kv_count))
    residual_slice = hidden.astype(jnp.float32) + shared
    total_sq = jnp.sum(gather_kv(jnp.sum(residual_slice * residual_slice, axis=1)), axis=0)
    gain_slice = lax.dynamic_slice_in_dim(gain_moe, kv_rank * slice_width, slice_width, 0)
    moe_slice_in = (
        residual_slice
        * lax.rsqrt(total_sq[:, None] / (slice_width * lax.axis_size("kv")) + epsilon)
        * gain_slice
    ).astype(jnp.bfloat16)
    top_count = routes.shape[1]
    blk_count = lax.axis_size("blk")
    blk_rank = lax.axis_index("blk")
    experts = EXP_DEV * blk_count
    capacity = max(2, 3 * tok_rows * top_count // (2 * experts))
    slots = experts * capacity
    pad = (-slice_width) % 128
    wide = slice_width + pad
    expert_ids, slot_ids = expert_slots(routes, experts)
    places = (expert_ids * capacity + slot_ids).reshape(tok_rows, top_count)
    slot_index = jnp.arange(slots, dtype=jnp.int32)
    picks = places[:, :, None] == slot_index[None, None, :]
    dispatch = jnp.any(picks, axis=1).astype(jnp.bfloat16)
    moe_wide = jnp.pad(moe_slice_in, ((0, 0), (0, pad)))
    outgoing = jnp.dot(dispatch.T, moe_wide, preferred_element_type=jnp.float32).astype(
        jnp.bfloat16
    )
    outgoing = outgoing.reshape(blk_count, EXP_DEV * capacity, wide)
    items = lax.all_to_all(outgoing, "blk", 0, 0, tiled=True)
    items = items.reshape(blk_count, EXP_DEV, capacity, wide).transpose(1, 0, 2, 3)
    items = items.reshape(EXP_DEV, blk_count * capacity, wide)
    gate_w = widen_rows(w_gate, kv_count, pad).reshape(EXP_DEV, kv_count, wide, -1)
    up_w = widen_rows(w_up, kv_count, pad).reshape(EXP_DEV, kv_count, wide, -1)
    down_w = widen_cols(w_down, kv_count, pad).reshape(EXP_DEV, -1, kv_count, wide)
    router_cols = lax.dynamic_slice_in_dim(w_router, blk_rank * EXP_DEV, EXP_DEV, 1)
    router_cols = widen_rows(router_cols.T[:, :, None], kv_count, pad)[:, :, 0]
    router_cols = router_cols.reshape(EXP_DEV, kv_count, wide)
    outs, chosen = [], []
    for el in range(EXP_DEV):
        with jax.named_scope(f"expert_{el}"):
            rows = gather_kv(items[el])
            gate_val = jnp.einsum("ird,idf->rf", rows, gate_w[el], preferred_element_type=jnp.float32)
            up_val = jnp.einsum("ird,idf->rf", rows, up_w[el], preferred_element_type=jnp.float32)
            act = swiglu(gate_val, up_val).astype(jnp.bfloat16)
            part = jnp.einsum(
                "rf,fid->ird", act, down_w[el], preferred_element_type=jnp.float32
            ).astype(jnp.bfloat16)
            outs.append(reduce_kv(part)[:, :slice_width].astype(jnp.bfloat16))
            chosen.append(
                jnp.einsum("ird,id->r", rows, router_cols[el], preferred_element_type=jnp.float32)
            )
    expert_out = jnp.concatenate(outs, axis=0)
    chosen = jnp.concatenate(chosen, axis=0).reshape(slots, 1)
    high = chosen.astype(jnp.bfloat16)
    rest = chosen - high.astype(jnp.float32)
    middle = rest.astype(jnp.bfloat16)
    low = (rest - middle.astype(jnp.float32)).astype(jnp.bfloat16)
    filler = jnp.zeros((slots, pad - 3), jnp.bfloat16)
    expert_out = jnp.concatenate([expert_out, high, middle, low, filler], axis=1)
    expert_out = expert_out.reshape(EXP_DEV, blk_count, capacity, wide).transpose(1, 0, 2, 3)
    expert_out = expert_out.reshape(blk_count, EXP_DEV * capacity, wide)
    arrived = lax.all_to_all(expert_out, "blk", 0, 0, tiled=True)
    arrived = arrived.reshape(slots, wide)
    picked = jnp.einsum(
        "tkp,pd->tkd", picks.astype(jnp.bfloat16), arrived, preferred_element_type=jnp.float32
    )
    logits = (
        picked[:, :, slice_width] + picked[:, :, slice_width + 1]
    ) + picked[:, :, slice_width + 2]
    weights = jax.nn.softmax(logits, axis=1)
    moe_slice = jnp.einsum("tk,tkd->td", weights, picked[:, :, :slice_width])
    return (residual_slice + moe_slice).astype(jnp.bfloat16)


def solution(mesh):
    in_specs = (
        P("blk", "kv"),
        P(),
        P(None, "kv"),
        P(None, "kv"),
        P(None, "kv"),
        P("kv"),
        P("kv", None),
        P(),
        P(),
        P("blk", None, "kv"),
        P("blk", None, "kv"),
        P("blk", "kv", None),
        P("blk", None, "kv"),
        P("blk", None),
        P("blk"),
        P("blk", None),
    )
    out_specs = P("blk", "kv")
    return jax.shard_map(local, mesh=mesh, in_specs=in_specs, out_specs=out_specs, check_vma=False)
```

```python
import jax
import jax.numpy as jnp
from jax import lax
from jax.sharding import PartitionSpec as P
from jax.experimental import pallas as pl
from jax.experimental.pallas import tpu as pltpu

HD = 64
EXP_DEV = 2


epsilon = 1e-05
rope_base = 150000.0
clamp_limit = 7.0
glu_alpha = 1.702


def rms_scale(values, gain_vec):
    mean_sq = jnp.mean(values * values, axis=-1, keepdims=True)
    return values * lax.rsqrt(mean_sq + epsilon) * gain_vec


def rotate(vectors, positions):
    half_dim = vectors.shape[-1] // 2
    inv_freq = rope_base ** (-jnp.arange(half_dim, dtype=jnp.float32) / half_dim)
    angles = positions.astype(jnp.float32)[:, None] * inv_freq[None, :]
    cosines = jnp.cos(angles)[:, None, :]
    sines = jnp.sin(angles)[:, None, :]
    front_half = vectors[..., :half_dim]
    back_half = vectors[..., half_dim:]
    return jnp.concatenate(
        [front_half * cosines - back_half * sines, back_half * cosines + front_half * sines],
        axis=-1,
    )


def swiglu(gate_in, up_in):
    gate_in = jnp.minimum(gate_in, clamp_limit)
    up_in = jnp.clip(up_in, -clamp_limit, clamp_limit)
    return (up_in + 1.0) * gate_in * jax.nn.sigmoid(glu_alpha * gate_in)


def head_kernel(len_ref, sink_ref, page_ref, q_ref, kn_ref, vn_ref, pool_ref, o_ref, pages, sems):
    head = pl.program_id(0)
    page_rows = pool_ref.shape[1]
    page_count = page_ref.shape[0]

    @pl.when(head == 0)
    def _():
        copies = [
            pltpu.make_async_copy(
                pool_ref.at[page_ref[i]], pages.at[pl.ds(i * page_rows, page_rows)], sems.at[i]
            )
            for i in range(page_count)
        ]
        for copy in copies:
            copy.start()
        for copy in copies:
            copy.wait()

    length = len_ref[0]
    query = q_ref[0]
    ctx_keys = pages[:, :HD]
    ctx_values = pages[:, HD:]
    dims = (((1,), (1,)), ((), ()))
    scale = HD ** (-0.5)
    s_ctx = lax.dot_general(query, ctx_keys, dims, preferred_element_type=jnp.float32) * scale
    s_new = lax.dot_general(query, kn_ref[...], dims, preferred_element_type=jnp.float32) * scale
    ctx_cols = lax.broadcasted_iota(jnp.int32, s_ctx.shape, 1)
    s_ctx = jnp.where(ctx_cols < length, s_ctx, -jnp.inf)
    new_rows = lax.broadcasted_iota(jnp.int32, s_new.shape, 0)
    new_cols = lax.broadcasted_iota(jnp.int32, s_new.shape, 1)
    s_new = jnp.where(new_cols <= new_rows, s_new, -jnp.inf)
    sink = sink_ref[head]
    row_top = jnp.maximum(
        jnp.maximum(jnp.max(s_ctx, axis=1, keepdims=True), jnp.max(s_new, axis=1, keepdims=True)),
        sink,
    )
    e_ctx = jnp.exp(s_ctx - row_top)
    e_new = jnp.exp(s_new - row_top)
    denom_sum = (
        jnp.sum(e_ctx, axis=1, keepdims=True) + jnp.sum(e_new, axis=1, keepdims=True)
    ) + jnp.exp(sink - row_top)
    p_ctx = (e_ctx / denom_sum).astype(jnp.bfloat16)
    p_new = (e_new / denom_sum).astype(jnp.bfloat16)
    out = jnp.dot(p_ctx, ctx_values, preferred_element_type=jnp.float32)
    out = out + jnp.dot(p_new, vn_ref[...], preferred_element_type=jnp.float32)
    o_ref[0] = out.astype(o_ref.dtype)


def attend(normed, length, page_ids, pool_all, w_q, w_k, w_v, sinks):
    tok_rows = normed.shape[0]
    heads = w_q.shape[1] // HD
    positions = length + jnp.arange(tok_rows, dtype=jnp.int32)
    queries = jnp.dot(normed, w_q, preferred_element_type=jnp.float32).reshape(tok_rows, heads, HD)
    queries = rotate(queries, positions).astype(jnp.bfloat16).transpose(1, 0, 2)
    key_new = jnp.dot(normed, w_k, preferred_element_type=jnp.float32).reshape(tok_rows, 1, HD)
    key_new = rotate(key_new, positions).astype(jnp.bfloat16).reshape(tok_rows, HD)
    value_new = jnp.dot(normed, w_v, preferred_element_type=jnp.float32).astype(jnp.bfloat16)
    page_count = page_ids.shape[0]
    page_rows, page_width = pool_all.shape[1], pool_all.shape[2]
    keys = page_count * page_rows + tok_rows
    attended = pl.pallas_call(
        head_kernel,
        out_shape=jax.ShapeDtypeStruct((heads, tok_rows, HD), jnp.bfloat16),
        grid_spec=pltpu.PrefetchScalarGridSpec(
            num_scalar_prefetch=3,
            grid=(heads,),
            in_specs=[
                pl.BlockSpec((1, tok_rows, HD), lambda h, n, s, t: (h, 0, 0)),
                pl.BlockSpec((tok_rows, HD), lambda h, n, s, t: (0, 0)),
                pl.BlockSpec((tok_rows, HD), lambda h, n, s, t: (0, 0)),
                pl.BlockSpec(memory_space=pl.ANY),
            ],
            out_specs=pl.BlockSpec((1, tok_rows, HD), lambda h, n, s, t: (h, 0, 0)),
            scratch_shapes=[
                pltpu.VMEM((page_count * page_rows, page_width), jnp.bfloat16),
                pltpu.SemaphoreType.DMA((page_count,)),
            ],
        ),
        compiler_params=pltpu.CompilerParams(dimension_semantics=("arbitrary",)),
        cost_estimate=pl.CostEstimate(
            flops=4 * heads * tok_rows * keys * HD,
            transcendentals=heads * tok_rows * keys,
            bytes_accessed=2 * (2 * heads * tok_rows * HD + 2 * keys * HD),
        ),
    )(length.reshape(1), sinks, page_ids, queries, key_new, value_new, pool_all)
    return attended.transpose(1, 0, 2).reshape(tok_rows, heads * HD)


def expert_slots(route_rows, expert_count):
    expert_ids = route_rows.reshape(-1)
    one_hot = (expert_ids[:, None] == jnp.arange(expert_count, dtype=jnp.int32)[None, :]).astype(
        jnp.int32
    )
    earlier = jnp.cumsum(one_hot, axis=0) - one_hot
    return (expert_ids, jnp.sum(earlier * one_hot, axis=1))


def gather_kv(block):
    count = lax.axis_size("kv")
    spread = jnp.broadcast_to(block[None], (count,) + block.shape)
    return lax.all_to_all(spread, "kv", 0, 0, tiled=True)


def reduce_kv(stacked):
    parts = lax.all_to_all(stacked, "kv", 0, 0, tiled=True)
    return jnp.sum(parts.astype(jnp.float32), axis=0)


def split_columns(block, count):
    rows, width = block.shape
    return block.reshape(rows, count, width // count).transpose(1, 0, 2)


def join_columns(stacked):
    count, rows, width = stacked.shape
    return stacked.transpose(1, 0, 2).reshape(rows, count * width)


def widen_rows(weight, count, pad):
    lead, depth, width = weight.shape
    weight = weight.reshape(lead, count, depth // count, width)
    weight = jnp.pad(weight, ((0, 0), (0, 0), (0, pad), (0, 0)))
    return weight.reshape(lead, count * (depth // count + pad), width)


def widen_cols(weight, count, pad):
    lead, depth, width = weight.shape
    weight = weight.reshape(lead, depth, count, width // count)
    weight = jnp.pad(weight, ((0, 0), (0, 0), (0, 0), (0, pad)))
    return weight.reshape(lead, depth, count * (width // count + pad))


def local(
    hidden,
    gain_attn,
    w_q,
    w_k,
    w_v,
    sinks,
    w_o,
    gain_moe,
    w_router,
    w_gate,
    w_up,
    w_down,
    kv_pool,
    page_table,
    lengths,
    routes,
):
    tok_rows = hidden.shape[0]
    slice_width = hidden.shape[1]
    kv_rank = lax.axis_index("kv")
    kv_count = lax.axis_size("kv")
    full_rows = join_columns(gather_kv(hidden))
    states = full_rows.astype(jnp.float32)
    normed = rms_scale(states, gain_attn).astype(jnp.bfloat16)
    pool_all = lax.all_gather(kv_pool, "blk", axis=0, tiled=True)
    attended = attend(normed, lengths[0], page_table[0], pool_all, w_q, w_k, w_v, sinks)
    partial_value = jnp.dot(attended, w_o, preferred_element_type=jnp.float32)
    shared = reduce_kv(split_columns(partial_value.astype(jnp.bfloat16), kv_count))
    residual_slice = hidden.astype(jnp.float32) + shared
    total_sq = jnp.sum(gather_kv(jnp.sum(residual_slice * residual_slice, axis=1)), axis=0)
    gain_slice = lax.dynamic_slice_in_dim(gain_moe, kv_rank * slice_width, slice_width, 0)
    moe_slice_in = (
        residual_slice
        * lax.rsqrt(total_sq[:, None] / (slice_width * lax.axis_size("kv")) + epsilon)
        * gain_slice
    ).astype(jnp.bfloat16)
    top_count = routes.shape[1]
    blk_count = lax.axis_size("blk")
    blk_rank = lax.axis_index("blk")
    experts = EXP_DEV * blk_count
    capacity = max(2, 3 * tok_rows * top_count // (2 * experts))
    slots = experts * capacity
    pad = (-slice_width) % 128
    wide = slice_width + pad
    expert_ids, slot_ids = expert_slots(routes, experts)
    places = (expert_ids * capacity + slot_ids).reshape(tok_rows, top_count)
    slot_index = jnp.arange(slots, dtype=jnp.int32)
    picks = places[:, :, None] == slot_index[None, None, :]
    dispatch = jnp.any(picks, axis=1).astype(jnp.bfloat16)
    moe_wide = jnp.pad(moe_slice_in, ((0, 0), (0, pad)))
    outgoing = jnp.dot(dispatch.T, moe_wide, preferred_element_type=jnp.float32).astype(
        jnp.bfloat16
    )
    outgoing = outgoing.reshape(blk_count, EXP_DEV * capacity, wide)
    items = lax.all_to_all(outgoing, "blk", 0, 0, tiled=True)
    items = items.reshape(blk_count, EXP_DEV, capacity, wide).transpose(1, 0, 2, 3)
    items = items.reshape(EXP_DEV, blk_count * capacity, wide)
    gate_w = widen_rows(w_gate, kv_count, pad).reshape(EXP_DEV, kv_count, wide, -1)
    up_w = widen_rows(w_up, kv_count, pad).reshape(EXP_DEV, kv_count, wide, -1)
    down_w = widen_cols(w_down, kv_count, pad).reshape(EXP_DEV, -1, kv_count, wide)
    router_cols = lax.dynamic_slice_in_dim(w_router, blk_rank * EXP_DEV, EXP_DEV, 1)
    router_cols = widen_rows(router_cols.T[:, :, None], kv_count, pad)[:, :, 0]
    router_cols = router_cols.reshape(EXP_DEV, kv_count, wide)
    outs, chosen = [], []
    for el in range(EXP_DEV):
        with jax.named_scope(f"expert_{el}"):
            rows = gather_kv(items[el])
            gate_val = jnp.einsum("ird,idf->rf", rows, gate_w[el], preferred_element_type=jnp.float32)
            up_val = jnp.einsum("ird,idf->rf", rows, up_w[el], preferred_element_type=jnp.float32)
            act = swiglu(gate_val, up_val).astype(jnp.bfloat16)
            part = jnp.einsum(
                "rf,fid->ird", act, down_w[el], preferred_element_type=jnp.float32
            ).astype(jnp.bfloat16)
            outs.append(reduce_kv(part)[:, :slice_width].astype(jnp.bfloat16))
            chosen.append(
                jnp.einsum("ird,id->r", rows, router_cols[el], preferred_element_type=jnp.float32)
            )
    expert_out = jnp.concatenate(outs, axis=0)
    chosen = jnp.concatenate(chosen, axis=0).reshape(slots, 1)
    high = chosen.astype(jnp.bfloat16)
    rest = chosen - high.astype(jnp.float32)
    middle = rest.astype(jnp.bfloat16)
    low = (rest - middle.astype(jnp.float32)).astype(jnp.bfloat16)
    filler = jnp.zeros((slots, pad - 3), jnp.bfloat16)
    expert_out = jnp.concatenate([expert_out, high, middle, low, filler], axis=1)
    expert_out = expert_out.reshape(EXP_DEV, blk_count, capacity, wide).transpose(1, 0, 2, 3)
    expert_out = expert_out.reshape(blk_count, EXP_DEV * capacity, wide)
    arrived = lax.all_to_all(expert_out, "blk", 0, 0, tiled=True)
    arrived = arrived.reshape(slots, wide)
    picked = jnp.einsum(
        "tkp,pd->tkd", picks.astype(jnp.bfloat16), arrived, preferred_element_type=jnp.float32
    )
    logits = (
        picked[:, :, slice_width] + picked[:, :, slice_width + 1]
    ) + picked[:, :, slice_width + 2]
    weights = jax.nn.softmax(logits, axis=1)
    moe_slice = jnp.einsum("tk,tkd->td", weights, picked[:, :, :slice_width])
    return (residual_slice + moe_slice).astype(jnp.bfloat16)


def solution(mesh):
    in_specs = (
        P("blk", "kv"),
        P(),
        P(None, "kv"),
        P(None, "kv"),
        P(None, "kv"),
        P("kv"),
        P("kv", None),
        P(),
        P(),
        P("blk", None, "kv"),
        P("blk", None, "kv"),
        P("blk", "kv", None),
        P("blk", None, "kv"),
        P("blk", None),
        P("blk"),
        P("blk", None),
    )
    out_specs = P("blk", "kv")
    return jax.shard_map(local, mesh=mesh, in_specs=in_specs, out_specs=out_specs, check_vma=False)
```

```python
import jax
import jax.numpy as jnp
from jax import lax
from jax.sharding import PartitionSpec as P
from jax.experimental import pallas as pl
from jax.experimental.pallas import tpu as pltpu

HD = 64
EXP_DEV = 2


epsilon = 1e-05
rope_base = 150000.0
clamp_limit = 7.0
glu_alpha = 1.702


def rms_scale(values, gain_vec):
    mean_sq = jnp.mean(values * values, axis=-1, keepdims=True)
    return values * lax.rsqrt(mean_sq + epsilon) * gain_vec


def rotate(vectors, positions):
    half_dim = vectors.shape[-1] // 2
    inv_freq = rope_base ** (-jnp.arange(half_dim, dtype=jnp.float32) / half_dim)
    angles = positions.astype(jnp.float32)[:, None] * inv_freq[None, :]
    cosines = jnp.cos(angles)[:, None, :]
    sines = jnp.sin(angles)[:, None, :]
    front_half = vectors[..., :half_dim]
    back_half = vectors[..., half_dim:]
    return jnp.concatenate(
        [front_half * cosines - back_half * sines, back_half * cosines + front_half * sines],
        axis=-1,
    )


def swiglu(gate_in, up_in):
    gate_in = jnp.minimum(gate_in, clamp_limit)
    up_in = jnp.clip(up_in, -clamp_limit, clamp_limit)
    return (up_in + 1.0) * gate_in * jax.nn.sigmoid(glu_alpha * gate_in)


def head_kernel(
    len_ref, sink_ref, page_ref, q_ref, kn_ref, vn_ref, pool_ref, wo_ref, o_ref, pages, sems, total
):
    head = pl.program_id(0)
    page_rows = pool_ref.shape[1]
    page_count = page_ref.shape[0]

    @pl.when(head == 0)
    def _():
        copies = [
            pltpu.make_async_copy(
                pool_ref.at[page_ref[i]], pages.at[pl.ds(i * page_rows, page_rows)], sems.at[i]
            )
            for i in range(page_count)
        ]
        for copy in copies:
            copy.start()
        for copy in copies:
            copy.wait()

    length = len_ref[0]
    query = q_ref[0]
    ctx_keys = pages[:, :HD]
    ctx_values = pages[:, HD:]
    dims = (((1,), (1,)), ((), ()))
    scale = HD ** (-0.5)
    s_ctx = lax.dot_general(query, ctx_keys, dims, preferred_element_type=jnp.float32) * scale
    s_new = lax.dot_general(query, kn_ref[...], dims, preferred_element_type=jnp.float32) * scale
    ctx_cols = lax.broadcasted_iota(jnp.int32, s_ctx.shape, 1)
    s_ctx = jnp.where(ctx_cols < length, s_ctx, -jnp.inf)
    new_rows = lax.broadcasted_iota(jnp.int32, s_new.shape, 0)
    new_cols = lax.broadcasted_iota(jnp.int32, s_new.shape, 1)
    s_new = jnp.where(new_cols <= new_rows, s_new, -jnp.inf)
    sink = sink_ref[head]
    row_top = jnp.maximum(
        jnp.maximum(jnp.max(s_ctx, axis=1, keepdims=True), jnp.max(s_new, axis=1, keepdims=True)),
        sink,
    )
    e_ctx = jnp.exp(s_ctx - row_top)
    e_new = jnp.exp(s_new - row_top)
    denom_sum = (
        jnp.sum(e_ctx, axis=1, keepdims=True) + jnp.sum(e_new, axis=1, keepdims=True)
    ) + jnp.exp(sink - row_top)
    p_ctx = (e_ctx / denom_sum).astype(jnp.bfloat16)
    p_new = (e_new / denom_sum).astype(jnp.bfloat16)
    out = jnp.dot(p_ctx, ctx_values, preferred_element_type=jnp.float32)
    out = out + jnp.dot(p_new, vn_ref[...], preferred_element_type=jnp.float32)
    rows = wo_ref[pl.ds(pl.multiple_of(head * HD, HD), HD), :]
    step = jnp.dot(out.astype(jnp.bfloat16), rows, preferred_element_type=jnp.float32)

    @pl.when(head == 0)
    def _():
        total[...] = step

    @pl.when(head > 0)
    def _():
        total[...] += step

    @pl.when(head == pl.num_programs(0) - 1)
    def _():
        o_ref[...] = total[...].astype(o_ref.dtype)


def attend(normed, length, page_ids, pool_all, w_q, w_k, w_v, sinks, w_o):
    tok_rows = normed.shape[0]
    heads = w_q.shape[1] // HD
    positions = length + jnp.arange(tok_rows, dtype=jnp.int32)
    queries = jnp.dot(normed, w_q, preferred_element_type=jnp.float32).reshape(tok_rows, heads, HD)
    queries = rotate(queries, positions).astype(jnp.bfloat16).transpose(1, 0, 2)
    key_new = jnp.dot(normed, w_k, preferred_element_type=jnp.float32).reshape(tok_rows, 1, HD)
    key_new = rotate(key_new, positions).astype(jnp.bfloat16).reshape(tok_rows, HD)
    value_new = jnp.dot(normed, w_v, preferred_element_type=jnp.float32).astype(jnp.bfloat16)
    page_count = page_ids.shape[0]
    page_rows, page_width = pool_all.shape[1], pool_all.shape[2]
    keys = page_count * page_rows + tok_rows
    attended = pl.pallas_call(
        head_kernel,
        out_shape=jax.ShapeDtypeStruct((tok_rows, w_o.shape[1]), jnp.bfloat16),
        grid_spec=pltpu.PrefetchScalarGridSpec(
            num_scalar_prefetch=3,
            grid=(heads,),
            in_specs=[
                pl.BlockSpec((1, tok_rows, HD), lambda h, n, s, t: (h, 0, 0)),
                pl.BlockSpec((tok_rows, HD), lambda h, n, s, t: (0, 0)),
                pl.BlockSpec((tok_rows, HD), lambda h, n, s, t: (0, 0)),
                pl.BlockSpec(memory_space=pl.ANY),
                pl.BlockSpec(w_o.shape, lambda h, n, s, t: (0, 0)),
            ],
            out_specs=pl.BlockSpec((tok_rows, w_o.shape[1]), lambda h, n, s, t: (0, 0)),
            scratch_shapes=[
                pltpu.VMEM((page_count * page_rows, page_width), jnp.bfloat16),
                pltpu.SemaphoreType.DMA((page_count,)),
                pltpu.VMEM((tok_rows, w_o.shape[1]), jnp.float32),
            ],
        ),
        compiler_params=pltpu.CompilerParams(dimension_semantics=("arbitrary",)),
        cost_estimate=pl.CostEstimate(
            flops=4 * heads * tok_rows * keys * HD,
            transcendentals=heads * tok_rows * keys,
            bytes_accessed=2 * (2 * heads * tok_rows * HD + 2 * keys * HD),
        ),
    )(length.reshape(1), sinks, page_ids, queries, key_new, value_new, pool_all, w_o)
    return attended


def expert_slots(route_rows, expert_count):
    expert_ids = route_rows.reshape(-1)
    one_hot = (expert_ids[:, None] == jnp.arange(expert_count, dtype=jnp.int32)[None, :]).astype(
        jnp.int32
    )
    earlier = jnp.cumsum(one_hot, axis=0) - one_hot
    return (expert_ids, jnp.sum(earlier * one_hot, axis=1))


def gather_kv(block):
    count = lax.axis_size("kv")
    spread = jnp.broadcast_to(block[None], (count,) + block.shape)
    return lax.all_to_all(spread, "kv", 0, 0, tiled=True)


def reduce_kv(stacked):
    parts = lax.all_to_all(stacked, "kv", 0, 0, tiled=True)
    return jnp.sum(parts.astype(jnp.float32), axis=0)


def split_columns(block, count):
    rows, width = block.shape
    return block.reshape(rows, count, width // count).transpose(1, 0, 2)


def join_columns(stacked):
    count, rows, width = stacked.shape
    return stacked.transpose(1, 0, 2).reshape(rows, count * width)


def widen_rows(weight, count, pad):
    lead, depth, width = weight.shape
    weight = weight.reshape(lead, count, depth // count, width)
    weight = jnp.pad(weight, ((0, 0), (0, 0), (0, pad), (0, 0)))
    return weight.reshape(lead, count * (depth // count + pad), width)


def widen_cols(weight, count, pad):
    lead, depth, width = weight.shape
    weight = weight.reshape(lead, depth, count, width // count)
    weight = jnp.pad(weight, ((0, 0), (0, 0), (0, 0), (0, pad)))
    return weight.reshape(lead, depth, count * (width // count + pad))


def local(
    hidden,
    gain_attn,
    w_q,
    w_k,
    w_v,
    sinks,
    w_o,
    gain_moe,
    w_router,
    w_gate,
    w_up,
    w_down,
    kv_pool,
    page_table,
    lengths,
    routes,
):
    tok_rows = hidden.shape[0]
    slice_width = hidden.shape[1]
    kv_rank = lax.axis_index("kv")
    kv_count = lax.axis_size("kv")
    full_rows = join_columns(gather_kv(hidden))
    states = full_rows.astype(jnp.float32)
    normed = rms_scale(states, gain_attn).astype(jnp.bfloat16)
    pool_all = lax.all_gather(kv_pool, "blk", axis=0, tiled=True)
    partial_value = attend(normed, lengths[0], page_table[0], pool_all, w_q, w_k, w_v, sinks, w_o)
    shared = reduce_kv(split_columns(partial_value, kv_count))
    residual_slice = hidden.astype(jnp.float32) + shared
    total_sq = jnp.sum(gather_kv(jnp.sum(residual_slice * residual_slice, axis=1)), axis=0)
    gain_slice = lax.dynamic_slice_in_dim(gain_moe, kv_rank * slice_width, slice_width, 0)
    moe_slice_in = (
        residual_slice
        * lax.rsqrt(total_sq[:, None] / (slice_width * lax.axis_size("kv")) + epsilon)
        * gain_slice
    ).astype(jnp.bfloat16)
    top_count = routes.shape[1]
    blk_count = lax.axis_size("blk")
    blk_rank = lax.axis_index("blk")
    experts = EXP_DEV * blk_count
    capacity = max(2, 3 * tok_rows * top_count // (2 * experts))
    slots = experts * capacity
    pad = (-slice_width) % 128
    wide = slice_width + pad
    expert_ids, slot_ids = expert_slots(routes, experts)
    places = (expert_ids * capacity + slot_ids).reshape(tok_rows, top_count)
    slot_index = jnp.arange(slots, dtype=jnp.int32)
    picks = places[:, :, None] == slot_index[None, None, :]
    dispatch = jnp.any(picks, axis=1).astype(jnp.bfloat16)
    moe_wide = jnp.pad(moe_slice_in, ((0, 0), (0, pad)))
    outgoing = jnp.dot(dispatch.T, moe_wide, preferred_element_type=jnp.float32).astype(
        jnp.bfloat16
    )
    outgoing = outgoing.reshape(blk_count, EXP_DEV * capacity, wide)
    items = lax.all_to_all(outgoing, "blk", 0, 0, tiled=True)
    items = items.reshape(blk_count, EXP_DEV, capacity, wide).transpose(1, 0, 2, 3)
    items = items.reshape(EXP_DEV, blk_count * capacity, wide)
    gate_w = widen_rows(w_gate, kv_count, pad).reshape(EXP_DEV, kv_count, wide, -1)
    up_w = widen_rows(w_up, kv_count, pad).reshape(EXP_DEV, kv_count, wide, -1)
    down_w = widen_cols(w_down, kv_count, pad).reshape(EXP_DEV, -1, kv_count, wide)
    router_cols = lax.dynamic_slice_in_dim(w_router, blk_rank * EXP_DEV, EXP_DEV, 1)
    router_cols = widen_rows(router_cols.T[:, :, None], kv_count, pad)[:, :, 0]
    router_cols = router_cols.reshape(EXP_DEV, kv_count, wide)
    outs, chosen = [], []
    for el in range(EXP_DEV):
        with jax.named_scope(f"expert_{el}"):
            rows = gather_kv(items[el])
            gate_val = jnp.einsum("ird,idf->rf", rows, gate_w[el], preferred_element_type=jnp.float32)
            up_val = jnp.einsum("ird,idf->rf", rows, up_w[el], preferred_element_type=jnp.float32)
            act = swiglu(gate_val, up_val).astype(jnp.bfloat16)
            part = jnp.einsum(
                "rf,fid->ird", act, down_w[el], preferred_element_type=jnp.float32
            ).astype(jnp.bfloat16)
            outs.append(reduce_kv(part)[:, :slice_width].astype(jnp.bfloat16))
            chosen.append(
                jnp.einsum("ird,id->r", rows, router_cols[el], preferred_element_type=jnp.float32)
            )
    expert_out = jnp.concatenate(outs, axis=0)
    chosen = jnp.concatenate(chosen, axis=0).reshape(slots, 1)
    high = chosen.astype(jnp.bfloat16)
    rest = chosen - high.astype(jnp.float32)
    middle = rest.astype(jnp.bfloat16)
    low = (rest - middle.astype(jnp.float32)).astype(jnp.bfloat16)
    filler = jnp.zeros((slots, pad - 3), jnp.bfloat16)
    expert_out = jnp.concatenate([expert_out, high, middle, low, filler], axis=1)
    expert_out = expert_out.reshape(EXP_DEV, blk_count, capacity, wide).transpose(1, 0, 2, 3)
    expert_out = expert_out.reshape(blk_count, EXP_DEV * capacity, wide)
    arrived = lax.all_to_all(expert_out, "blk", 0, 0, tiled=True)
    arrived = arrived.reshape(slots, wide)
    picked = jnp.einsum(
        "tkp,pd->tkd", picks.astype(jnp.bfloat16), arrived, preferred_element_type=jnp.float32
    )
    logits = (
        picked[:, :, slice_width] + picked[:, :, slice_width + 1]
    ) + picked[:, :, slice_width + 2]
    weights = jax.nn.softmax(logits, axis=1)
    moe_slice = jnp.einsum("tk,tkd->td", weights, picked[:, :, :slice_width])
    return (residual_slice + moe_slice).astype(jnp.bfloat16)


def solution(mesh):
    in_specs = (
        P("blk", "kv"),
        P(),
        P(None, "kv"),
        P(None, "kv"),
        P(None, "kv"),
        P("kv"),
        P("kv", None),
        P(),
        P(),
        P("blk", None, "kv"),
        P("blk", None, "kv"),
        P("blk", "kv", None),
        P("blk", None, "kv"),
        P("blk", None),
        P("blk"),
        P("blk", None),
    )
    out_specs = P("blk", "kv")
    return jax.shard_map(local, mesh=mesh, in_specs=in_specs, out_specs=out_specs, check_vma=False)
```
